128 devices in a mesh: grp: 4 (over x), seq: 32 (over y, z, core).
Axes of the slice: x: 4, y: 4, z: 4, core: 2. Of those that a mesh axis runs over, the one named last changes fastest.
Arguments:
- grad_output: bfloat16 [4096, 8192], P('seq', 'grp'), may hold values from -6 to 6
- hidden: bfloat16 [4096, 28672], P('seq', 'grp'), may hold values from -6 to 6
- down_weight: bfloat16 [28672, 8192], P('seq', 'grp'), may hold values from -0.0625 to 0.0625
- adapter_down: bfloat16 [64, 64, 28672], P(None, None, ('grp', 'seq')), may hold values from -0.03125 to 0.03125
- adapter_up: bfloat16 [64, 64, 8192], P(None, None, ('grp', 'seq')), may hold values from -0.0625 to 0.0625
- job_tenant: int32 [32, 4], replicated, may hold values from 0 to 63, all different within a row
- job_count: int32 [32, 4], replicated, may hold values from 1 to 64, 128 in all within a row
Outputs:
- grad_hidden: bfloat16 [4096, 28672], P('seq', 'grp')
- grad_adapter_down: float32 [64, 64, 28672], P(None, None, ('grp', 'seq'))
- grad_adapter_up: float32 [64, 64, 8192], P(None, None, ('grp', 'seq'))
The draws below stay inside these ranges and needn't reach their ends.
Inputs may be any that keep to these rules, and one draw needn't show every extreme that they name: `job_tenant`: each row names 4 different tenants; every tenant is named by some row. `job_count`: each row sums to 128, and its largest entry is exactly 64.
All inputs are finite; a program needn't handle non-finite values.
Results may differ from the reference program's by a relative error of at most 0.015.
Values may be sent and summed in bfloat16 or wider, within the bound.
A program may use at most 128 MiB of HBM per device.

```python
import math
import jax
import jax.numpy as jnp
import numpy as np
from jax import lax

D = 8192
FF = 28672
R = 64
TOK_DEV = 128
JOBS = 4
JOB_MOST = 64
TOKENS = 4096
TENANTS = 64
N_GRP = 4
N_SEQ = 32


def block_scale(stream_key, dims, shards, least, top_value):
    factor_of, own = 1.0, jax.random.fold_in(stream_key, 6)
    for axis_at, parts in shards:
        draws = jnp.exp(jax.random.uniform(jax.random.fold_in(own, axis_at), (parts,), jnp.float32, least / len(shards), top_value / len(shards)))
        factor_of = factor_of * jnp.repeat(draws, dims[axis_at] // parts).reshape([-1 if axis == axis_at else 1 for axis in range(len(dims))])
    return factor_of


def picks_of(key, rows, number_of, top, lift):
    ranking = jax.random.permutation(jax.random.fold_in(key, 1), number_of)
    favour = ranking
    for power in range(3):
        favour = favour * favour // number_of
    favour = favour * lift // number_of
    chance = jax.random.randint(jax.random.fold_in(key, 2), (rows, number_of), 0, 4096) + favour
    holders = jax.random.permutation(jax.random.fold_in(key, 3), rows)[jnp.arange(number_of) % rows]
    chance = jnp.where(jnp.arange(rows)[:, None] == holders[None, :], 1 << 14, chance)
    score = chance * number_of + jnp.arange(number_of)
    return lax.top_k(score.astype(jnp.int32), top)[1].astype(jnp.int32)


def split_up(number_of, total, reach, slope):
    portions = [(1 << 20) // math.isqrt(rank ** slope) + 1 for rank in range(2, number_of + 1)]
    surplus, given = total - reach - (number_of - 1), [1] * (number_of - 1)
    while surplus > 0:
        movable = [i for i in range(number_of - 1) if given[i] < reach]
        pool, budget = sum([portions[i] for i in movable]), surplus
        for i in movable:
            addition = min(reach - given[i], max(1, budget * portions[i] // pool), surplus)
            given[i] = given[i] + addition
            surplus = surplus - addition
    return np.array([reach] + given)


def ragged_sizes(stream_key, number_of, total, limit, lean):
    if number_of == 2:
        one = jax.random.randint(stream_key, (), max(1, total - limit), min(limit, total - 1) + 1)
        return jnp.stack([one, total - one])
    tallies = jnp.asarray(split_up(number_of, total, limit, lean), jnp.int32)
    pairs = (number_of - 1) // 2
    donor, taker = tallies[1:1 + 2 * pairs:2], tallies[2:2 + 2 * pairs:2]
    margin = jnp.minimum(donor - 1, limit - taker)
    shifted = jax.random.randint(jax.random.fold_in(stream_key, 1), (pairs,), 0, 1 << 20) % (margin + 1)
    tallies = tallies.at[1:1 + 2 * pairs:2].set(donor - shifted).at[2:2 + 2 * pairs:2].set(taker + shifted)
    return tallies[jax.random.permutation(jax.random.fold_in(stream_key, 2), number_of)]


def scatter_about(stream_key, dims, width, limit, shards=(), held_as=jnp.bfloat16):
    loudness = block_scale(stream_key, dims, shards, -0.22, 0.18) if shards else 1.0
    result = jax.random.normal(stream_key, dims, jnp.float32) * width * loudness
    return jnp.minimum(jnp.maximum(result, -limit), limit).astype(held_as)


def setup_inputs(seed: int = 0) -> dict:
    splits = jax.random.split(jax.random.key(seed), 8)
    grad_output = scatter_about(splits[0], (TOKENS, D), 1.0, 6.0, ((0, 32), (1, 4)))
    hidden = scatter_about(splits[1], (TOKENS, FF), 1.0, 6.0, ((0, 32), (1, 4)))
    down_weight = scatter_about(splits[2], (FF, D), D ** -0.5, 0.0625, ((0, 32), (1, 4)))
    adapter_down = scatter_about(splits[3], (TENANTS, R, FF), FF ** -0.5, 0.03125, ((2, 128),))
    adapter_up = scatter_about(splits[4], (TENANTS, R, D), D ** -0.5, 0.0625, ((2, 128),))
    job_tenant = picks_of(splits[5], N_SEQ, TENANTS, JOBS, 1024)
    job_count = jax.vmap(lambda own: ragged_sizes(own, JOBS, TOK_DEV, JOB_MOST, 1))(jax.random.split(splits[6], N_SEQ)).reshape((N_SEQ, JOBS)).astype(jnp.int32)
    return {"grad_output": grad_output, "hidden": hidden, "down_weight": down_weight, "adapter_down": adapter_down, "adapter_up": adapter_up, "job_tenant": job_tenant, "job_count": job_count}


ADAPTER_SCALE = 2.0


def settle(value):
    return lax.optimization_barrier(value.astype(jnp.bfloat16)).astype(jnp.float32)


def reference(grad_output, hidden, down_weight, adapter_down, adapter_up, job_tenant, job_count):
    width_d = D // N_GRP
    width_f = FF // N_GRP
    base_sum = jnp.zeros((TOKENS, FF), jnp.float32)
    for group in range(N_GRP):
        columns = slice(group * width_d, (group + 1) * width_d)
        partial_value = lax.dot_general(grad_output[:, columns], down_weight[:, columns],
                                  (((1,), (1,)), ((), ())), preferred_element_type=jnp.float32)
        base_sum = base_sum + settle(partial_value)
    base_grad = base_sum.astype(jnp.bfloat16)

    tenant_table = (job_tenant[:, :, None] == jnp.arange(TENANTS, dtype=jnp.int32)[None, None, :]).astype(jnp.float32)
    totals = jnp.sum(job_count.astype(jnp.float32)[:, :, None] * tenant_table, axis=(0, 1))
    weights = ADAPTER_SCALE / totals
    positions = jnp.arange(TOK_DEV, dtype=jnp.int32)

    def shard(carry, inputs):
        grad_down, grad_up = carry
        rows_out, rows_hidden, rows_base, tenants, counts = inputs
        run_ends = jnp.cumsum(counts)
        run_starts = run_ends - counts
        member = ((positions[:, None] >= run_starts[None, :]) & (positions[:, None] < run_ends[None, :])).astype(jnp.float32)
        down_sel = adapter_down[tenants].astype(jnp.float32)
        up_sel = adapter_up[tenants].astype(jnp.float32)
        out_rows = rows_out.astype(jnp.float32)
        hid_rows = rows_hidden.astype(jnp.float32)
        grad_rank = jnp.zeros((TOK_DEV, R), jnp.float32)
        act_rank = jnp.zeros((TOK_DEV, R), jnp.float32)
        for group in range(N_GRP):
            dcolumns = slice(group * width_d, (group + 1) * width_d)
            fcolumns = slice(group * width_f, (group + 1) * width_f)
            grad_proj = jnp.einsum("td,jrd->tjr", out_rows[:, dcolumns], up_sel[:, :, dcolumns])
            act_proj = jnp.einsum("tf,jrf->tjr", hid_rows[:, fcolumns], down_sel[:, :, fcolumns])
            grad_rank = grad_rank + settle(jnp.sum(grad_proj * member[:, :, None], axis=1))
            act_rank = act_rank + settle(jnp.sum(act_proj * member[:, :, None], axis=1))
        grad_spread = member[:, :, None] * settle(grad_rank)[:, None, :]
        act_spread = member[:, :, None] * settle(act_rank)[:, None, :]
        adapter_term = ADAPTER_SCALE * jnp.einsum("tjr,jrf->tf", grad_spread, down_sel)
        rows_grad = (rows_base.astype(jnp.float32) + adapter_term).astype(jnp.bfloat16)
        job_weights = weights[tenants]
        part_down = settle(job_weights[:, None, None] * jnp.einsum("tjr,tf->jrf", grad_spread, hid_rows))
        part_up = settle(job_weights[:, None, None] * jnp.einsum("tjr,td->jrd", act_spread, out_rows))
        grad_down = grad_down.at[tenants].add(part_down)
        grad_up = grad_up.at[tenants].add(part_up)
        return (grad_down, grad_up), rows_grad

    start = (jnp.zeros((TENANTS, R, FF), jnp.float32), jnp.zeros((TENANTS, R, D), jnp.float32))
    inputs = (grad_output.reshape(N_SEQ, TOK_DEV, D), hidden.reshape(N_SEQ, TOK_DEV, FF),
              base_grad.reshape(N_SEQ, TOK_DEV, FF), job_tenant, job_count)
    (grad_down, grad_up), rows = lax.scan(shard, start, inputs)
    return rows.reshape(TOKENS, FF), grad_down, grad_up
```

```python
import jax
import jax.numpy as jnp
from jax import lax
from jax.sharding import PartitionSpec as P

ADAPTER_SCALE = 2.0


def shards(grad_output, hidden, down_weight, adapter_down, adapter_up, job_tenant, job_count):
    shard_index = lax.axis_index(SEQ)
    shard_count = lax.axis_size(SEQ)
    group_count = lax.axis_size("grp")
    tok_rows = grad_output.shape[0]
    job_slots = job_tenant.shape[1]
    ranks = adapter_down.shape[1]
    down_slab = adapter_down.shape[2]
    up_slab = adapter_up.shape[2]
    tenant_total = adapter_down.shape[0]
    contract_last = (((1,), (1,)), ((), ()))
    contract_rows = (((0,), (0,)), ((), ()))
    tenant_table = (
        job_tenant[:, :, None] == lax.broadcasted_iota(jnp.int32, (1, 1, tenant_total), 2)
    ).astype(jnp.float32)
    totals = jnp.sum(job_count.astype(jnp.float32)[:, :, None] * tenant_table, axis=(0, 1))
    weights = ADAPTER_SCALE / totals
    table_here = lax.dynamic_index_in_dim(tenant_table, shard_index, 0, keepdims=False)
    job_weights = jnp.sum(table_here * weights[None, :], axis=1)
    counts_here = lax.dynamic_index_in_dim(job_count, shard_index, 0, keepdims=False)
    run_ends = jnp.cumsum(counts_here)
    run_starts = run_ends - counts_here
    positions = lax.broadcasted_iota(jnp.int32, (tok_rows, job_slots), 0)
    member = ((positions >= run_starts[None, :]) & (positions < run_ends[None, :])).astype(
        jnp.float32
    )
    chosen = job_tenant.T
    fetched_down, fetched_up = (
        lax.all_to_all(adapter_down[chosen], SEQ, split_axis=1, concat_axis=3, tiled=True),
        lax.all_to_all(adapter_up[chosen], SEQ, split_axis=1, concat_axis=3, tiled=True),
    )
    down_stack = fetched_down.reshape(job_slots * ranks, shard_count * down_slab)
    up_stack = fetched_up.reshape(job_slots * ranks, shard_count * up_slab)

    def select_jobs(projected):
        return jnp.sum(projected.reshape(tok_rows, job_slots, ranks) * member[:, :, None], axis=1)

    grad_proj = lax.dot_general(
        grad_output, up_stack, contract_last, preferred_element_type=jnp.float32
    )
    act_proj = lax.dot_general(
        hidden, down_stack, contract_last, preferred_element_type=jnp.float32
    )
    rank_part = jnp.concatenate([select_jobs(grad_proj), select_jobs(act_proj)], axis=1).astype(
        jnp.bfloat16
    )
    weight_pair = lax.all_gather(down_weight, "core", axis=0, tiled=True)
    tokens_same_core = lax.all_gather(grad_output, "chip", axis=0, tiled=True)
    partial_value = lax.dot_general(
        tokens_same_core, weight_pair, contract_last, preferred_element_type=jnp.float32
    )
    routed = lax.all_to_all(
        partial_value.astype(jnp.bfloat16), "chip", split_axis=0, concat_axis=1, tiled=True
    )
    width_here = routed.shape[1] // group_count
    base_grad = lax.psum_scatter(
        routed.reshape(tok_rows, group_count, width_here), "grp", scatter_dimension=1, tiled=True
    ).reshape(tok_rows, width_here)
    rank_sum = lax.psum(rank_part.astype(jnp.float32), "grp")
    grad_rank = rank_sum[:, :ranks].astype(jnp.bfloat16)
    act_rank = rank_sum[:, ranks:].astype(jnp.bfloat16)
    grad_spread = (
        (member[:, :, None] * lax.optimization_barrier(grad_rank).astype(jnp.float32)[:, None, :])
        .reshape(tok_rows, job_slots * ranks)
        .astype(jnp.bfloat16)
    )
    act_spread = (
        (member[:, :, None] * lax.optimization_barrier(act_rank).astype(jnp.float32)[:, None, :])
        .reshape(tok_rows, job_slots * ranks)
        .astype(jnp.bfloat16)
    )
    adapter_term = (
        jnp.dot(grad_spread, down_stack, preferred_element_type=jnp.float32) * ADAPTER_SCALE
    )
    grad_hidden = (base_grad.astype(jnp.float32) + adapter_term).astype(jnp.bfloat16)
    down_rows = lax.dot_general(
        grad_spread, hidden, contract_rows, preferred_element_type=jnp.float32
    )
    down_rows = (down_rows.reshape(job_slots, ranks, -1) * job_weights[:, None, None]).astype(
        jnp.bfloat16
    )
    up_rows = lax.dot_general(
        act_spread, grad_output, contract_rows, preferred_element_type=jnp.float32
    )
    up_rows = (up_rows.reshape(job_slots, ranks, -1) * job_weights[:, None, None]).astype(
        jnp.bfloat16
    )
    returned_down, returned_up = (
        lax.all_to_all(
            down_rows.reshape(job_slots, ranks, shard_count, down_slab),
            SEQ,
            split_axis=2,
            concat_axis=1,
            tiled=True,
        ),
        lax.all_to_all(
            up_rows.reshape(job_slots, ranks, shard_count, up_slab),
            SEQ,
            split_axis=2,
            concat_axis=1,
            tiled=True,
        ),
    )
    tenant_map = (
        tenant_table.transpose(1, 0, 2)
        .reshape(job_slots * shard_count, tenant_total)
        .astype(jnp.bfloat16)
    )
    grad_adapter_down = lax.dot_general(
        tenant_map,
        returned_down.reshape(job_slots * shard_count, ranks * down_slab),
        contract_rows,
        preferred_element_type=jnp.float32,
    ).reshape(tenant_total, ranks, down_slab)
    grad_adapter_up = lax.dot_general(
        tenant_map,
        returned_up.reshape(job_slots * shard_count, ranks * up_slab),
        contract_rows,
        preferred_element_type=jnp.float32,
    ).reshape(tenant_total, ranks, up_slab)
    return (grad_hidden, grad_adapter_down, grad_adapter_up)


SEQ = ("chip", "core")


def solution(mesh):
    chips = mesh.devices.reshape(mesh.shape["grp"], mesh.shape["seq"] // 2, 2)
    mesh = jax.sharding.Mesh(chips, ("grp", "chip", "core"))
    placed = (
        P(SEQ, "grp"),
        P(SEQ, "grp"),
        P(SEQ, "grp"),
        P(None, None, ("grp", "chip", "core")),
        P(None, None, ("grp", "chip", "core")),
        P(),
        P(),
    )
    return jax.shard_map(
        shards,
        mesh=mesh,
        in_specs=placed,
        out_specs=(P(SEQ, "grp"), P(None, None, ("grp", "chip", "core")), P(None, None, ("grp", "chip", "core"))),
        check_vma=False,
    )
```

```python
import jax
import jax.numpy as jnp
from jax import lax
from jax.sharding import PartitionSpec as P

ADAPTER_SCALE = 2.0


def shards(grad_output, hidden, down_weight, adapter_down, adapter_up, job_tenant, job_count):
    shard_index = lax.axis_index(SEQ)
    shard_count = lax.axis_size(SEQ)
    group_count = lax.axis_size("grp")
    tok_rows = grad_output.shape[0]
    job_slots = job_tenant.shape[1]
    ranks = adapter_down.shape[1]
    down_slab = adapter_down.shape[2]
    up_slab = adapter_up.shape[2]
    tenant_total = adapter_down.shape[0]
    contract_last = (((1,), (1,)), ((), ()))
    contract_rows = (((0,), (0,)), ((), ()))
    tenant_table = (
        job_tenant[:, :, None] == lax.broadcasted_iota(jnp.int32, (1, 1, tenant_total), 2)
    ).astype(jnp.float32)
    totals = jnp.sum(job_count.astype(jnp.float32)[:, :, None] * tenant_table, axis=(0, 1))
    weights = ADAPTER_SCALE / totals
    table_here = lax.dynamic_index_in_dim(tenant_table, shard_index, 0, keepdims=False)
    job_weights = jnp.sum(table_here * weights[None, :], axis=1)
    counts_here = lax.dynamic_index_in_dim(job_count, shard_index, 0, keepdims=False)
    run_ends = jnp.cumsum(counts_here)
    run_starts = run_ends - counts_here
    positions = lax.broadcasted_iota(jnp.int32, (tok_rows, job_slots), 0)
    member = ((positions >= run_starts[None, :]) & (positions < run_ends[None, :])).astype(
        jnp.float32
    )
    chosen = job_tenant.T
    fetched_down, fetched_up = (
        lax.all_to_all(adapter_down[chosen], SEQ, split_axis=1, concat_axis=3, tiled=True),
        lax.all_to_all(adapter_up[chosen], SEQ, split_axis=1, concat_axis=3, tiled=True),
    )
    down_stack = fetched_down.reshape(job_slots * ranks, shard_count * down_slab)
    up_stack = fetched_up.reshape(job_slots * ranks, shard_count * up_slab)

    def select_jobs(projected):
        return jnp.sum(projected.reshape(tok_rows, job_slots, ranks) * member[:, :, None], axis=1)

    grad_proj = lax.dot_general(
        grad_output, up_stack, contract_last, preferred_element_type=jnp.float32
    )
    act_proj = lax.dot_general(
        hidden, down_stack, contract_last, preferred_element_type=jnp.float32
    )
    rank_part = jnp.concatenate([select_jobs(grad_proj), select_jobs(act_proj)], axis=1).astype(
        jnp.bfloat16
    )
    weight_pair = lax.all_gather(down_weight, "core", axis=0, tiled=True)
    tokens_same_core = lax.all_gather(grad_output, "chip", axis=0, tiled=True)
    tokens_same_core, weight_pair, rank_part = lax.optimization_barrier(
        (tokens_same_core, weight_pair, rank_part)
    )
    partial_value = lax.dot_general(
        tokens_same_core, weight_pair, contract_last, preferred_element_type=jnp.float32
    )
    quarter = lax.psum_scatter(
        partial_value.astype(jnp.bfloat16), "grp", scatter_dimension=0, tiled=True
    )
    quarter = quarter.reshape(group_count, tok_rows, quarter.shape[1])
    chip_count = lax.axis_size("chip")
    row_of_chip = chip_count // group_count
    chip = lax.axis_index("chip")
    group = lax.axis_index("grp")
    core = lax.axis_index("core")
    lane = chip % row_of_chip
    arrived = []
    for step in range(group_count):
        piece = lax.dynamic_index_in_dim(quarter, (lane + step) % group_count, 0, keepdims=False)
        pairs = []
        for g in range(group_count):
            for c in range(chip_count):
                for k in range(2):
                    z = c % row_of_chip
                    dest_chip = g * row_of_chip + (z + step) % group_count
                    dest_group = c // row_of_chip
                    pairs.append(((g * chip_count + c) * 2 + k, (dest_group * chip_count + dest_chip) * 2 + k))
        arrived.append(lax.ppermute(piece, ("grp", "chip", "core"), pairs))
    arrived = jnp.stack(arrived)
    order = (lane - jnp.arange(group_count)) % group_count
    base_grad = jnp.take(arrived, order, axis=0).transpose(1, 0, 2).reshape(tok_rows, -1)
    rank_sum = lax.psum(rank_part.astype(jnp.float32), "grp")
    grad_rank = rank_sum[:, :ranks].astype(jnp.bfloat16)
    act_rank = rank_sum[:, ranks:].astype(jnp.bfloat16)
    grad_spread = (
        (member[:, :, None] * lax.optimization_barrier(grad_rank).astype(jnp.float32)[:, None, :])
        .reshape(tok_rows, job_slots * ranks)
        .astype(jnp.bfloat16)
    )
    act_spread = (
        (member[:, :, None] * lax.optimization_barrier(act_rank).astype(jnp.float32)[:, None, :])
        .reshape(tok_rows, job_slots * ranks)
        .astype(jnp.bfloat16)
    )
    adapter_term = (
        jnp.dot(grad_spread, down_stack, preferred_element_type=jnp.float32) * ADAPTER_SCALE
    )
    grad_hidden = (base_grad.astype(jnp.float32) + adapter_term).astype(jnp.bfloat16)
    down_rows = lax.dot_general(
        grad_spread, hidden, contract_rows, preferred_element_type=jnp.float32
    )
    down_rows = (down_rows.reshape(job_slots, ranks, -1) * job_weights[:, None, None]).astype(
        jnp.bfloat16
    )
    up_rows = lax.dot_general(
        act_spread, grad_output, contract_rows, preferred_element_type=jnp.float32
    )
    up_rows = (up_rows.reshape(job_slots, ranks, -1) * job_weights[:, None, None]).astype(
        jnp.bfloat16
    )
    returned_down, returned_up = (
        lax.all_to_all(
            down_rows.reshape(job_slots, ranks, shard_count, down_slab),
            SEQ,
            split_axis=2,
            concat_axis=1,
            tiled=True,
        ),
        lax.all_to_all(
            up_rows.reshape(job_slots, ranks, shard_count, up_slab),
            SEQ,
            split_axis=2,
            concat_axis=1,
            tiled=True,
        ),
    )
    tenant_map = (
        tenant_table.transpose(1, 0, 2)
        .reshape(job_slots * shard_count, tenant_total)
        .astype(jnp.bfloat16)
    )
    grad_adapter_down = lax.dot_general(
        tenant_map,
        returned_down.reshape(job_slots * shard_count, ranks * down_slab),
        contract_rows,
        preferred_element_type=jnp.float32,
    ).reshape(tenant_total, ranks, down_slab)
    grad_adapter_up = lax.dot_general(
        tenant_map,
        returned_up.reshape(job_slots * shard_count, ranks * up_slab),
        contract_rows,
        preferred_element_type=jnp.float32,
    ).reshape(tenant_total, ranks, up_slab)
    return (grad_hidden, grad_adapter_down, grad_adapter_up)


SEQ = ("chip", "core")


def solution(mesh):
    chips = mesh.devices.reshape(mesh.shape["grp"], mesh.shape["seq"] // 2, 2)
    mesh = jax.sharding.Mesh(chips, ("grp", "chip", "core"))
    placed = (
        P(SEQ, "grp"),
        P(SEQ, "grp"),
        P(SEQ, "grp"),
        P(None, None, ("grp", "chip", "core")),
        P(None, None, ("grp", "chip", "core")),
        P(),
        P(),
    )
    return jax.shard_map(
        shards,
        mesh=mesh,
        in_specs=placed,
        out_specs=(P(SEQ, "grp"), P(None, None, ("grp", "chip", "core")), P(None, None, ("grp", "chip", "core"))),
        check_vma=False,
    )
```

```python
import jax
import jax.numpy as jnp
from jax import lax
from jax.sharding import PartitionSpec as P

ADAPTER_SCALE = 2.0


def shards(grad_output, hidden, down_weight, adapter_down, adapter_up, job_tenant, job_count):
    shard_index = lax.axis_index(SEQ)
    shard_count = lax.axis_size(SEQ)
    group_count = lax.axis_size("grp")
    tok_rows = grad_output.shape[0]
    job_slots = job_tenant.shape[1]
    ranks = adapter_down.shape[1]
    down_slab = adapter_down.shape[2]
    up_slab = adapter_up.shape[2]
    tenant_total = adapter_down.shape[0]
    contract_last = (((1,), (1,)), ((), ()))
    contract_rows = (((0,), (0,)), ((), ()))
    tenant_table = (
        job_tenant[:, :, None] == lax.broadcasted_iota(jnp.int32, (1, 1, tenant_total), 2)
    ).astype(jnp.float32)
    totals = jnp.sum(job_count.astype(jnp.float32)[:, :, None] * tenant_table, axis=(0, 1))
    weights = ADAPTER_SCALE / totals
    table_here = lax.dynamic_index_in_dim(tenant_table, shard_index, 0, keepdims=False)
    job_weights = jnp.sum(table_here * weights[None, :], axis=1)
    counts_here = lax.dynamic_index_in_dim(job_count, shard_index, 0, keepdims=False)
    run_ends = jnp.cumsum(counts_here)
    run_starts = run_ends - counts_here
    positions = lax.broadcasted_iota(jnp.int32, (tok_rows, job_slots), 0)
    member = ((positions >= run_starts[None, :]) & (positions < run_ends[None, :])).astype(
        jnp.float32
    )
    hidden_cols = lax.all_to_all(
        hidden.reshape(tok_rows, shard_count, down_slab), SEQ, split_axis=1, concat_axis=0, tiled=True
    ).reshape(shard_count, tok_rows, down_slab)
    output_cols = lax.all_to_all(
        grad_output.reshape(tok_rows, shard_count, up_slab), SEQ, split_axis=1, concat_axis=0, tiled=True
    ).reshape(shard_count, tok_rows, up_slab)
    chosen = job_tenant.T
    fetched_down, fetched_up = (
        lax.all_to_all(adapter_down[chosen], SEQ, split_axis=1, concat_axis=3, tiled=True),
        lax.all_to_all(adapter_up[chosen], SEQ, split_axis=1, concat_axis=3, tiled=True),
    )
    down_stack = fetched_down.reshape(job_slots * ranks, shard_count * down_slab)
    up_stack = fetched_up.reshape(job_slots * ranks, shard_count * up_slab)

    def select_jobs(projected):
        return jnp.sum(projected.reshape(tok_rows, job_slots, ranks) * member[:, :, None], axis=1)

    grad_proj = lax.dot_general(
        grad_output, up_stack, contract_last, preferred_element_type=jnp.float32
    )
    act_proj = lax.dot_general(
        hidden, down_stack, contract_last, preferred_element_type=jnp.float32
    )
    rank_part = jnp.concatenate([select_jobs(grad_proj), select_jobs(act_proj)], axis=1).astype(
        jnp.bfloat16
    )
    weight_pair = lax.all_gather(down_weight, "core", axis=0, tiled=True)
    tokens_same_core = lax.all_gather(grad_output, "chip", axis=0, tiled=True)
    tokens_same_core, weight_pair, rank_part = lax.optimization_barrier(
        (tokens_same_core, weight_pair, rank_part)
    )
    partial_value = lax.dot_general(
        tokens_same_core, weight_pair, contract_last, preferred_element_type=jnp.float32
    )
    quarter = lax.psum_scatter(
        partial_value.astype(jnp.bfloat16), "grp", scatter_dimension=0, tiled=True
    )
    quarter = quarter.reshape(group_count, tok_rows, quarter.shape[1])
    chip_count = lax.axis_size("chip")
    row_of_chip = chip_count // group_count
    chip = lax.axis_index("chip")
    group = lax.axis_index("grp")
    core = lax.axis_index("core")
    lane = chip % row_of_chip
    arrived = []
    for step in range(group_count):
        piece = lax.dynamic_index_in_dim(quarter, (lane + step) % group_count, 0, keepdims=False)
        pairs = []
        for g in range(group_count):
            for c in range(chip_count):
                for k in range(2):
                    z = c % row_of_chip
                    dest_chip = g * row_of_chip + (z + step) % group_count
                    dest_group = c // row_of_chip
                    pairs.append(((g * chip_count + c) * 2 + k, (dest_group * chip_count + dest_chip) * 2 + k))
        arrived.append(lax.ppermute(piece, ("grp", "chip", "core"), pairs))
    arrived = jnp.stack(arrived)
    order = (lane - jnp.arange(group_count)) % group_count
    base_grad = jnp.take(arrived, order, axis=0).transpose(1, 0, 2).reshape(tok_rows, -1)
    rank_sum = lax.psum(rank_part.astype(jnp.float32), "grp")
    grad_rank = rank_sum[:, :ranks].astype(jnp.bfloat16)
    act_rank = rank_sum[:, ranks:].astype(jnp.bfloat16)
    grad_spread = (
        (member[:, :, None] * lax.optimization_barrier(grad_rank).astype(jnp.float32)[:, None, :])
        .reshape(tok_rows, job_slots * ranks)
        .astype(jnp.bfloat16)
    )
    adapter_term = (
        jnp.dot(grad_spread, down_stack, preferred_element_type=jnp.float32) * ADAPTER_SCALE
    )
    grad_hidden = (base_grad.astype(jnp.float32) + adapter_term).astype(jnp.bfloat16)

    all_positions = lax.broadcasted_iota(jnp.int32, (shard_count, tok_rows, job_slots), 1)
    all_ends = jnp.cumsum(job_count, axis=1)
    all_starts = all_ends - job_count
    member_all = (
        (all_positions >= all_starts[:, None, :]) & (all_positions < all_ends[:, None, :])
    ).astype(jnp.float32)
    weight_all = jnp.sum(tenant_table * weights[None, None, :], axis=2)
    rank_all = lax.all_gather(
        jnp.concatenate([grad_rank, act_rank], axis=1), SEQ, axis=0, tiled=True
    ).astype(jnp.float32).reshape(shard_count, tok_rows, 1, 2 * ranks)
    tenant_map = (
        tenant_table.reshape(shard_count * job_slots, tenant_total).astype(jnp.bfloat16)
    )

    def adapter_grad(rank_rows, columns):
        spread = (member_all[:, :, :, None] * rank_rows).astype(jnp.bfloat16)
        per_job = jnp.einsum(
            "stjr,stc->sjrc", spread, columns, preferred_element_type=jnp.float32
        )
        per_job = (per_job * weight_all[:, :, None, None]).astype(jnp.bfloat16)
        slab = per_job.shape[-1]
        return lax.dot_general(
            tenant_map,
            per_job.reshape(shard_count * job_slots, ranks * slab),
            contract_rows,
            preferred_element_type=jnp.float32,
        ).reshape(tenant_total, ranks, slab)

    grad_adapter_down = adapter_grad(rank_all[..., :ranks], hidden_cols)
    grad_adapter_up = adapter_grad(rank_all[..., ranks:], output_cols)
    return (grad_hidden, grad_adapter_down, grad_adapter_up)


SEQ = ("chip", "core")


def solution(mesh):
    chips = mesh.devices.reshape(mesh.shape["grp"], mesh.shape["seq"] // 2, 2)
    mesh = jax.sharding.Mesh(chips, ("grp", "chip", "core"))
    placed = (
        P(SEQ, "grp"),
        P(SEQ, "grp"),
        P(SEQ, "grp"),
        P(None, None, ("grp", "chip", "core")),
        P(None, None, ("grp", "chip", "core")),
        P(),
        P(),
    )
    return jax.shard_map(
        shards,
        mesh=mesh,
        in_specs=placed,
        out_specs=(P(SEQ, "grp"), P(None, None, ("grp", "chip", "core")), P(None, None, ("grp", "chip", "core"))),
        check_vma=False,
    )
```

```python
import jax
import jax.numpy as jnp
from jax import lax
from jax.sharding import PartitionSpec as P

ADAPTER_SCALE = 2.0


def shards(grad_output, hidden, down_weight, adapter_down, adapter_up, job_tenant, job_count):
    shard_index = lax.axis_index(SEQ)
    shard_count = lax.axis_size(SEQ)
    group_count = lax.axis_size("grp")
    tok_rows = grad_output.shape[0]
    job_slots = job_tenant.shape[1]
    ranks = adapter_down.shape[1]
    down_slab = adapter_down.shape[2]
    up_slab = adapter_up.shape[2]
    tenant_total = adapter_down.shape[0]
    contract_last = (((1,), (1,)), ((), ()))
    contract_rows = (((0,), (0,)), ((), ()))
    tenant_table = (
        job_tenant[:, :, None] == lax.broadcasted_iota(jnp.int32, (1, 1, tenant_total), 2)
    ).astype(jnp.float32)
    totals = jnp.sum(job_count.astype(jnp.float32)[:, :, None] * tenant_table, axis=(0, 1))
    weights = ADAPTER_SCALE / totals
    table_here = lax.dynamic_index_in_dim(tenant_table, shard_index, 0, keepdims=False)
    job_weights = jnp.sum(table_here * weights[None, :], axis=1)
    counts_here = lax.dynamic_index_in_dim(job_count, shard_index, 0, keepdims=False)
    run_ends = jnp.cumsum(counts_here)
    run_starts = run_ends - counts_here
    positions = lax.broadcasted_iota(jnp.int32, (tok_rows, job_slots), 0)
    member = ((positions >= run_starts[None, :]) & (positions < run_ends[None, :])).astype(
        jnp.float32
    )
    hidden_cols = lax.all_to_all(
        hidden.reshape(tok_rows, shard_count, down_slab), SEQ, split_axis=1, concat_axis=0, tiled=True
    ).reshape(shard_count, tok_rows, down_slab)
    output_cols = lax.all_to_all(
        grad_output.reshape(tok_rows, shard_count, up_slab), SEQ, split_axis=1, concat_axis=0, tiled=True
    ).reshape(shard_count, tok_rows, up_slab)
    chosen = job_tenant.T
    fetched_down, fetched_up = (
        lax.all_to_all(adapter_down[chosen], SEQ, split_axis=1, concat_axis=3, tiled=True),
        lax.all_to_all(adapter_up[chosen], SEQ, split_axis=1, concat_axis=3, tiled=True),
    )
    down_stack = fetched_down.reshape(job_slots * ranks, shard_count * down_slab)
    up_stack = fetched_up.reshape(job_slots * ranks, shard_count * up_slab)

    def select_jobs(projected):
        return jnp.sum(projected.reshape(tok_rows, job_slots, ranks) * member[:, :, None], axis=1)

    grad_proj = lax.dot_general(
        grad_output, up_stack, contract_last, preferred_element_type=jnp.float32
    )
    act_proj = lax.dot_general(
        hidden, down_stack, contract_last, preferred_element_type=jnp.float32
    )
    rank_part = jnp.concatenate([select_jobs(grad_proj), select_jobs(act_proj)], axis=1).astype(
        jnp.bfloat16
    )
    weight_pair = lax.all_gather(down_weight, "core", axis=0, tiled=True)
    tokens_same_core = lax.all_gather(grad_output, "chip", axis=0, tiled=True)
    rank_sum = lax.psum(rank_part.astype(jnp.float32), "grp")
    tokens_same_core, weight_pair, rank_sum = lax.optimization_barrier(
        (tokens_same_core, weight_pair, rank_sum)
    )
    partial_value = lax.dot_general(
        tokens_same_core, weight_pair, contract_last, preferred_element_type=jnp.float32
    )
    quarter = lax.psum_scatter(
        partial_value.astype(jnp.bfloat16), "grp", scatter_dimension=0, tiled=True
    )
    quarter = quarter.reshape(group_count, tok_rows, quarter.shape[1])
    quarter, rank_sum, hidden_cols, output_cols = lax.optimization_barrier(
        (quarter, rank_sum, hidden_cols, output_cols)
    )
    chip_count = lax.axis_size("chip")
    row_of_chip = chip_count // group_count
    chip = lax.axis_index("chip")
    group = lax.axis_index("grp")
    core = lax.axis_index("core")
    lane = chip % row_of_chip
    arrived = []
    for step in range(group_count):
        piece = lax.dynamic_index_in_dim(quarter, (lane + step) % group_count, 0, keepdims=False)
        pairs = []
        for g in range(group_count):
            for c in range(chip_count):
                for k in range(2):
                    z = c % row_of_chip
                    dest_chip = g * row_of_chip + (z + step) % group_count
                    dest_group = c // row_of_chip
                    pairs.append(((g * chip_count + c) * 2 + k, (dest_group * chip_count + dest_chip) * 2 + k))
        arrived.append(lax.ppermute(piece, ("grp", "chip", "core"), pairs))
    arrived = jnp.stack(arrived)
    order = (lane - jnp.arange(group_count)) % group_count
    base_grad = jnp.take(arrived, order, axis=0).transpose(1, 0, 2).reshape(tok_rows, -1)
    grad_rank = rank_sum[:, :ranks].astype(jnp.bfloat16)
    act_rank = rank_sum[:, ranks:].astype(jnp.bfloat16)
    grad_spread = (
        (member[:, :, None] * lax.optimization_barrier(grad_rank).astype(jnp.float32)[:, None, :])
        .reshape(tok_rows, job_slots * ranks)
        .astype(jnp.bfloat16)
    )
    adapter_term = (
        jnp.dot(grad_spread, down_stack, preferred_element_type=jnp.float32) * ADAPTER_SCALE
    )
    grad_hidden = (base_grad.astype(jnp.float32) + adapter_term).astype(jnp.bfloat16)

    all_positions = lax.broadcasted_iota(jnp.int32, (shard_count, tok_rows, job_slots), 1)
    all_ends = jnp.cumsum(job_count, axis=1)
    all_starts = all_ends - job_count
    member_all = (
        (all_positions >= all_starts[:, None, :]) & (all_positions < all_ends[:, None, :])
    ).astype(jnp.float32)
    weight_all = jnp.sum(tenant_table * weights[None, None, :], axis=2)
    rank_all = lax.all_gather(
        jnp.concatenate([grad_rank, act_rank], axis=1), SEQ, axis=0, tiled=True
    ).astype(jnp.float32).reshape(shard_count, tok_rows, 1, 2 * ranks)
    tenant_map = (
        tenant_table.reshape(shard_count * job_slots, tenant_total).astype(jnp.bfloat16)
    )

    def adapter_grad(rank_rows, columns):
        spread = (member_all[:, :, :, None] * rank_rows).astype(jnp.bfloat16)
        per_job = jnp.einsum(
            "stjr,stc->sjrc", spread, columns, preferred_element_type=jnp.float32
        )
        per_job = (per_job * weight_all[:, :, None, None]).astype(jnp.bfloat16)
        slab = per_job.shape[-1]
        return lax.dot_general(
            tenant_map,
            per_job.reshape(shard_count * job_slots, ranks * slab),
            contract_rows,
            preferred_element_type=jnp.float32,
        ).reshape(tenant_total, ranks, slab)

    grad_adapter_down = adapter_grad(rank_all[..., :ranks], hidden_cols)
    grad_adapter_up = adapter_grad(rank_all[..., ranks:], output_cols)
    return (grad_hidden, grad_adapter_down, grad_adapter_up)


SEQ = ("chip", "core")


def solution(mesh):
    chips = mesh.devices.reshape(mesh.shape["grp"], mesh.shape["seq"] // 2, 2)
    mesh = jax.sharding.Mesh(chips, ("grp", "chip", "core"))
    placed = (
        P(SEQ, "grp"),
        P(SEQ, "grp"),
        P(SEQ, "grp"),
        P(None, None, ("grp", "chip", "core")),
        P(None, None, ("grp", "chip", "core")),
        P(),
        P(),
    )
    return jax.shard_map(
        shards,
        mesh=mesh,
        in_specs=placed,
        out_specs=(P(SEQ, "grp"), P(None, None, ("grp", "chip", "core")), P(None, None, ("grp", "chip", "core"))),
        check_vma=False,
    )
```

```python
import jax
import jax.numpy as jnp
from jax import lax
from jax.sharding import PartitionSpec as P

ADAPTER_SCALE = 2.0


def shards(grad_output, hidden, down_weight, adapter_down, adapter_up, job_tenant, job_count):
    shard_index = lax.axis_index(SEQ)
    shard_count = lax.axis_size(SEQ)
    group_count = lax.axis_size("grp")
    tok_rows = grad_output.shape[0]
    job_slots = job_tenant.shape[1]
    ranks = adapter_down.shape[1]
    down_slab = adapter_down.shape[2]
    up_slab = adapter_up.shape[2]
    tenant_total = adapter_down.shape[0]
    contract_last = (((1,), (1,)), ((), ()))
    contract_rows = (((0,), (0,)), ((), ()))
    tenant_table = (
        job_tenant[:, :, None] == lax.broadcasted_iota(jnp.int32, (1, 1, tenant_total), 2)
    ).astype(jnp.float32)
    totals = jnp.sum(job_count.astype(jnp.float32)[:, :, None] * tenant_table, axis=(0, 1))
    weights = ADAPTER_SCALE / totals
    table_here = lax.dynamic_index_in_dim(tenant_table, shard_index, 0, keepdims=False)
    job_weights = jnp.sum(table_here * weights[None, :], axis=1)
    counts_here = lax.dynamic_index_in_dim(job_count, shard_index, 0, keepdims=False)
    run_ends = jnp.cumsum(counts_here)
    run_starts = run_ends - counts_here
    positions = lax.broadcasted_iota(jnp.int32, (tok_rows, job_slots), 0)
    member = ((positions >= run_starts[None, :]) & (positions < run_ends[None, :])).astype(
        jnp.float32
    )
    hidden_cols = lax.all_to_all(
        hidden.reshape(tok_rows, shard_count, down_slab), SEQ, split_axis=1, concat_axis=0, tiled=True
    ).reshape(shard_count, tok_rows, down_slab)
    output_cols = lax.all_to_all(
        grad_output.reshape(tok_rows, shard_count, up_slab), SEQ, split_axis=1, concat_axis=0, tiled=True
    ).reshape(shard_count, tok_rows, up_slab)
    chosen = job_tenant.T
    fetched_down, fetched_up = (
        lax.all_to_all(adapter_down[chosen], SEQ, split_axis=1, concat_axis=3, tiled=True),
        lax.all_to_all(adapter_up[chosen], SEQ, split_axis=1, concat_axis=3, tiled=True),
    )
    down_stack = fetched_down.reshape(job_slots * ranks, shard_count * down_slab)
    up_stack = fetched_up.reshape(job_slots * ranks, shard_count * up_slab)

    def select_jobs(projected):
        return jnp.sum(projected.reshape(tok_rows, job_slots, ranks) * member[:, :, None], axis=1)

    grad_proj = lax.dot_general(
        grad_output, up_stack, contract_last, preferred_element_type=jnp.float32
    )
    act_proj = lax.dot_general(
        hidden, down_stack, contract_last, preferred_element_type=jnp.float32
    )
    rank_part = jnp.concatenate([select_jobs(grad_proj), select_jobs(act_proj)], axis=1).astype(
        jnp.bfloat16
    )
    weight_pair = lax.all_gather(down_weight, "core", axis=0, tiled=True)
    tokens_same_core = lax.all_gather(grad_output, "chip", axis=0, tiled=True)
    rank_sum = lax.psum(rank_part.astype(jnp.float32), "grp")
    tokens_same_core, weight_pair, rank_sum = lax.optimization_barrier(
        (tokens_same_core, weight_pair, rank_sum)
    )
    partial_value = lax.dot_general(
        tokens_same_core, weight_pair, contract_last, preferred_element_type=jnp.float32
    )
    quarter = lax.psum_scatter(
        partial_value.astype(jnp.bfloat16), "grp", scatter_dimension=0, tiled=True
    )
    quarter = quarter.reshape(group_count, tok_rows, quarter.shape[1])
    quarter, hidden_cols, output_cols = lax.optimization_barrier(
        (quarter, hidden_cols, output_cols)
    )
    chip_count = lax.axis_size("chip")
    row_of_chip = chip_count // group_count
    chip = lax.axis_index("chip")
    group = lax.axis_index("grp")
    core = lax.axis_index("core")
    lane = chip % row_of_chip
    arrived = []
    for step in range(group_count):
        piece = lax.dynamic_index_in_dim(quarter, (lane + step) % group_count, 0, keepdims=False)
        pairs = []
        for g in range(group_count):
            for c in range(chip_count):
                for k in range(2):
                    z = c % row_of_chip
                    dest_chip = g * row_of_chip + (z + step) % group_count
                    dest_group = c // row_of_chip
                    pairs.append(((g * chip_count + c) * 2 + k, (dest_group * chip_count + dest_chip) * 2 + k))
        arrived.append(lax.ppermute(piece, ("grp", "chip", "core"), pairs))
    arrived = jnp.stack(arrived)
    order = (lane - jnp.arange(group_count)) % group_count
    base_grad = jnp.take(arrived, order, axis=0).transpose(1, 0, 2).reshape(tok_rows, -1)
    grad_rank = rank_sum[:, :ranks].astype(jnp.bfloat16)
    act_rank = rank_sum[:, ranks:].astype(jnp.bfloat16)
    grad_spread = (
        (member[:, :, None] * lax.optimization_barrier(grad_rank).astype(jnp.float32)[:, None, :])
        .reshape(tok_rows, job_slots * ranks)
        .astype(jnp.bfloat16)
    )
    adapter_term = (
        jnp.dot(grad_spread, down_stack, preferred_element_type=jnp.float32) * ADAPTER_SCALE
    )
    grad_hidden = (base_grad.astype(jnp.float32) + adapter_term).astype(jnp.bfloat16)

    all_positions = lax.broadcasted_iota(jnp.int32, (shard_count, tok_rows, job_slots), 1)
    all_ends = jnp.cumsum(job_count, axis=1)
    all_starts = all_ends - job_count
    member_all = (
        (all_positions >= all_starts[:, None, :]) & (all_positions < all_ends[:, None, :])
    ).astype(jnp.float32)
    weight_all = jnp.sum(tenant_table * weights[None, None, :], axis=2)
    rank_rows = jnp.concatenate([grad_rank, act_rank], axis=1)
    rank_all = lax.all_to_all(
        jnp.broadcast_to(rank_rows[None], (shard_count,) + rank_rows.shape),
        SEQ,
        split_axis=0,
        concat_axis=0,
        tiled=True,
    ).astype(jnp.float32).reshape(shard_count, tok_rows, 1, 2 * ranks)
    tenant_map = (
        tenant_table.reshape(shard_count * job_slots, tenant_total).astype(jnp.bfloat16)
    )

    def adapter_grad(rank_rows, columns):
        spread = (member_all[:, :, :, None] * rank_rows).astype(jnp.bfloat16)
        per_job = jnp.einsum(
            "stjr,stc->sjrc", spread, columns, preferred_element_type=jnp.float32
        )
        per_job = (per_job * weight_all[:, :, None, None]).astype(jnp.bfloat16)
        slab = per_job.shape[-1]
        return lax.dot_general(
            tenant_map,
            per_job.reshape(shard_count * job_slots, ranks * slab),
            contract_rows,
            preferred_element_type=jnp.float32,
        ).reshape(tenant_total, ranks, slab)

    grad_adapter_down = adapter_grad(rank_all[..., :ranks], hidden_cols)
    grad_adapter_up = adapter_grad(rank_all[..., ranks:], output_cols)
    return (grad_hidden, grad_adapter_down, grad_adapter_up)


SEQ = ("chip", "core")


def solution(mesh):
    chips = mesh.devices.reshape(mesh.shape["grp"], mesh.shape["seq"] // 2, 2)
    mesh = jax.sharding.Mesh(chips, ("grp", "chip", "core"))
    placed = (
        P(SEQ, "grp"),
        P(SEQ, "grp"),
        P(SEQ, "grp"),
        P(None, None, ("grp", "chip", "core")),
        P(None, None, ("grp", "chip", "core")),
        P(),
        P(),
    )
    return jax.shard_map(
        shards,
        mesh=mesh,
        in_specs=placed,
        out_specs=(P(SEQ, "grp"), P(None, None, ("grp", "chip", "core")), P(None, None, ("grp", "chip", "core"))),
        check_vma=False,
    )
```

```python
import jax
import jax.numpy as jnp
from jax import lax
from jax.sharding import PartitionSpec as P

ADAPTER_SCALE = 2.0


def shards(grad_output, hidden, down_weight, adapter_down, adapter_up, job_tenant, job_count):
    shard_index = lax.axis_index(SEQ)
    shard_count = lax.axis_size(SEQ)
    group_count = lax.axis_size("grp")
    tok_rows = grad_output.shape[0]
    job_slots = job_tenant.shape[1]
    ranks = adapter_down.shape[1]
    down_slab = adapter_down.shape[2]
    up_slab = adapter_up.shape[2]
    tenant_total = adapter_down.shape[0]
    contract_last = (((1,), (1,)), ((), ()))
    contract_rows = (((0,), (0,)), ((), ()))
    tenant_table = (
        job_tenant[:, :, None] == lax.broadcasted_iota(jnp.int32, (1, 1, tenant_total), 2)
    ).astype(jnp.float32)
    totals = jnp.sum(job_count.astype(jnp.float32)[:, :, None] * tenant_table, axis=(0, 1))
    weights = ADAPTER_SCALE / totals
    table_here = lax.dynamic_index_in_dim(tenant_table, shard_index, 0, keepdims=False)
    job_weights = jnp.sum(table_here * weights[None, :], axis=1)
    counts_here = lax.dynamic_index_in_dim(job_count, shard_index, 0, keepdims=False)
    run_ends = jnp.cumsum(counts_here)
    run_starts = run_ends - counts_here
    positions = lax.broadcasted_iota(jnp.int32, (tok_rows, job_slots), 0)
    member = ((positions >= run_starts[None, :]) & (positions < run_ends[None, :])).astype(
        jnp.float32
    )
    hidden_cols = lax.all_to_all(
        hidden.reshape(tok_rows, shard_count, down_slab), SEQ, split_axis=1, concat_axis=0, tiled=True
    ).reshape(shard_count, tok_rows, down_slab)
    output_cols = lax.all_to_all(
        grad_output.reshape(tok_rows, shard_count, up_slab), SEQ, split_axis=1, concat_axis=0, tiled=True
    ).reshape(shard_count, tok_rows, up_slab)
    chosen = job_tenant.T
    tokens_same_core = lax.all_gather(grad_output, "chip", axis=0, tiled=True)
    down_picked, up_picked, tokens_same_core = lax.optimization_barrier(
        (adapter_down[chosen], adapter_up[chosen], tokens_same_core)
    )
    fetched_down, fetched_up = (
        lax.all_to_all(down_picked, SEQ, split_axis=1, concat_axis=3, tiled=True),
        lax.all_to_all(up_picked, SEQ, split_axis=1, concat_axis=3, tiled=True),
    )
    down_stack = fetched_down.reshape(job_slots * ranks, shard_count * down_slab)
    up_stack = fetched_up.reshape(job_slots * ranks, shard_count * up_slab)

    def select_jobs(projected):
        return jnp.sum(projected.reshape(tok_rows, job_slots, ranks) * member[:, :, None], axis=1)

    grad_proj = lax.dot_general(
        grad_output, up_stack, contract_last, preferred_element_type=jnp.float32
    )
    act_proj = lax.dot_general(
        hidden, down_stack, contract_last, preferred_element_type=jnp.float32
    )
    rank_part = jnp.concatenate([select_jobs(grad_proj), select_jobs(act_proj)], axis=1).astype(
        jnp.bfloat16
    )
    partner_weight = lax.ppermute(down_weight, "core", [(0, 1), (1, 0)])
    on_first_core = lax.axis_index("core") == 0
    weight_pair = jnp.concatenate(
        [
            jnp.where(on_first_core, down_weight, partner_weight),
            jnp.where(on_first_core, partner_weight, down_weight),
        ],
        axis=0,
    )
    rank_sum = lax.psum(rank_part.astype(jnp.float32), "grp")
    partial_value = lax.dot_general(
        tokens_same_core, weight_pair, contract_last, preferred_element_type=jnp.float32
    )
    quarter = lax.psum_scatter(
        partial_value.astype(jnp.bfloat16), "grp", scatter_dimension=0, tiled=True
    )
    quarter = quarter.reshape(group_count, tok_rows, quarter.shape[1])
    quarter, hidden_cols, output_cols = lax.optimization_barrier(
        (quarter, hidden_cols, output_cols)
    )
    chip_count = lax.axis_size("chip")
    row_of_chip = chip_count // group_count
    chip = lax.axis_index("chip")
    group = lax.axis_index("grp")
    core = lax.axis_index("core")
    lane = chip % row_of_chip
    arrived = []
    for step in range(group_count):
        piece = lax.dynamic_index_in_dim(quarter, (lane + step) % group_count, 0, keepdims=False)
        pairs = []
        for g in range(group_count):
            for c in range(chip_count):
                for k in range(2):
                    z = c % row_of_chip
                    dest_chip = g * row_of_chip + (z + step) % group_count
                    dest_group = c // row_of_chip
                    pairs.append(((g * chip_count + c) * 2 + k, (dest_group * chip_count + dest_chip) * 2 + k))
        arrived.append(lax.ppermute(piece, ("grp", "chip", "core"), pairs))
    arrived = jnp.stack(arrived)
    order = (lane - jnp.arange(group_count)) % group_count
    base_grad = jnp.take(arrived, order, axis=0).transpose(1, 0, 2).reshape(tok_rows, -1)
    grad_rank = rank_sum[:, :ranks].astype(jnp.bfloat16)
    act_rank = rank_sum[:, ranks:].astype(jnp.bfloat16)
    grad_spread = (
        (member[:, :, None] * lax.optimization_barrier(grad_rank).astype(jnp.float32)[:, None, :])
        .reshape(tok_rows, job_slots * ranks)
        .astype(jnp.bfloat16)
    )
    adapter_term = (
        jnp.dot(grad_spread, down_stack, preferred_element_type=jnp.float32) * ADAPTER_SCALE
    )
    grad_hidden = (base_grad.astype(jnp.float32) + adapter_term).astype(jnp.bfloat16)

    all_positions = lax.broadcasted_iota(jnp.int32, (shard_count, tok_rows, job_slots), 1)
    all_ends = jnp.cumsum(job_count, axis=1)
    all_starts = all_ends - job_count
    member_all = (
        (all_positions >= all_starts[:, None, :]) & (all_positions < all_ends[:, None, :])
    ).astype(jnp.float32)
    weight_all = jnp.sum(tenant_table * weights[None, None, :], axis=2)
    rank_rows = jnp.concatenate([grad_rank, act_rank], axis=1)
    rank_all = lax.all_to_all(
        jnp.broadcast_to(rank_rows[None], (shard_count,) + rank_rows.shape),
        SEQ,
        split_axis=0,
        concat_axis=0,
        tiled=True,
    ).astype(jnp.float32).reshape(shard_count, tok_rows, 1, 2 * ranks)
    tenant_map = (
        tenant_table.reshape(shard_count * job_slots, tenant_total).astype(jnp.bfloat16)
    )

    def adapter_grad(rank_rows, columns):
        spread = (member_all[:, :, :, None] * rank_rows).astype(jnp.bfloat16)
        per_job = jnp.einsum(
            "stjr,stc->sjrc", spread, columns, preferred_element_type=jnp.float32
        )
        per_job = (per_job * weight_all[:, :, None, None]).astype(jnp.bfloat16)
        slab = per_job.shape[-1]
        return lax.dot_general(
            tenant_map,
            per_job.reshape(shard_count * job_slots, ranks * slab),
            contract_rows,
            preferred_element_type=jnp.float32,
        ).reshape(tenant_total, ranks, slab)

    grad_adapter_down = adapter_grad(rank_all[..., :ranks], hidden_cols)
    grad_adapter_up = adapter_grad(rank_all[..., ranks:], output_cols)
    return (grad_hidden, grad_adapter_down, grad_adapter_up)


SEQ = ("chip", "core")


def solution(mesh):
    chips = mesh.devices.reshape(mesh.shape["grp"], mesh.shape["seq"] // 2, 2)
    mesh = jax.sharding.Mesh(chips, ("grp", "chip", "core"))
    placed = (
        P(SEQ, "grp"),
        P(SEQ, "grp"),
        P(SEQ, "grp"),
        P(None, None, ("grp", "chip", "core")),
        P(None, None, ("grp", "chip", "core")),
        P(),
        P(),
    )
    return jax.shard_map(
        shards,
        mesh=mesh,
        in_specs=placed,
        out_specs=(P(SEQ, "grp"), P(None, None, ("grp", "chip", "core")), P(None, None, ("grp", "chip", "core"))),
        check_vma=False,
    )
```

```python
import jax
import jax.numpy as jnp
from jax import lax
from jax.sharding import PartitionSpec as P

ADAPTER_SCALE = 2.0


def shards(grad_output, hidden, down_weight, adapter_down, adapter_up, job_tenant, job_count):
    shard_index = lax.axis_index(SEQ)
    shard_count = lax.axis_size(SEQ)
    group_count = lax.axis_size("grp")
    tok_rows = grad_output.shape[0]
    job_slots = job_tenant.shape[1]
    ranks = adapter_down.shape[1]
    down_slab = adapter_down.shape[2]
    up_slab = adapter_up.shape[2]
    tenant_total = adapter_down.shape[0]
    contract_last = (((1,), (1,)), ((), ()))
    contract_rows = (((0,), (0,)), ((), ()))
    tenant_table = (
        job_tenant[:, :, None] == lax.broadcasted_iota(jnp.int32, (1, 1, tenant_total), 2)
    ).astype(jnp.float32)
    totals = jnp.sum(job_count.astype(jnp.float32)[:, :, None] * tenant_table, axis=(0, 1))
    weights = ADAPTER_SCALE / totals
    table_here = lax.dynamic_index_in_dim(tenant_table, shard_index, 0, keepdims=False)
    job_weights = jnp.sum(table_here * weights[None, :], axis=1)
    counts_here = lax.dynamic_index_in_dim(job_count, shard_index, 0, keepdims=False)
    run_ends = jnp.cumsum(counts_here)
    run_starts = run_ends - counts_here
    positions = lax.broadcasted_iota(jnp.int32, (tok_rows, job_slots), 0)
    member = ((positions >= run_starts[None, :]) & (positions < run_ends[None, :])).astype(
        jnp.float32
    )
    chosen = job_tenant.T
    tokens_same_core = lax.all_gather(grad_output, "chip", axis=0, tiled=True)
    down_picked, up_picked, hidden_moved, output_moved, tokens_same_core = lax.optimization_barrier(
        (adapter_down[chosen], adapter_up[chosen], hidden, grad_output, tokens_same_core)
    )
    hidden_cols = lax.all_to_all(
        hidden_moved.reshape(tok_rows, shard_count, down_slab), SEQ, split_axis=1, concat_axis=0, tiled=True
    ).reshape(shard_count, tok_rows, down_slab)
    output_cols = lax.all_to_all(
        output_moved.reshape(tok_rows, shard_count, up_slab), SEQ, split_axis=1, concat_axis=0, tiled=True
    ).reshape(shard_count, tok_rows, up_slab)
    fetched_down, fetched_up = (
        lax.all_to_all(down_picked, SEQ, split_axis=1, concat_axis=3, tiled=True),
        lax.all_to_all(up_picked, SEQ, split_axis=1, concat_axis=3, tiled=True),
    )
    down_stack = fetched_down.reshape(job_slots * ranks, shard_count * down_slab)
    up_stack = fetched_up.reshape(job_slots * ranks, shard_count * up_slab)

    partner_weight = lax.ppermute(down_weight, "core", [(0, 1), (1, 0)])
    on_first_core = lax.axis_index("core") == 0
    weight_pair = jnp.concatenate(
        [
            jnp.where(on_first_core, down_weight, partner_weight),
            jnp.where(on_first_core, partner_weight, down_weight),
        ],
        axis=0,
    )
    partial_value = lax.dot_general(
        tokens_same_core, weight_pair, contract_last, preferred_element_type=jnp.float32
    )
    quarter = lax.psum_scatter(
        partial_value.astype(jnp.bfloat16), "grp", scatter_dimension=0, tiled=True
    )
    quarter = quarter.reshape(group_count, tok_rows, quarter.shape[1])
    down_stack, up_stack, hidden_cols, output_cols, quarter = lax.optimization_barrier(
        (down_stack, up_stack, hidden_cols, output_cols, quarter)
    )
    def select_jobs(projected):
        return jnp.sum(projected.reshape(tok_rows, job_slots, ranks) * member[:, :, None], axis=1)

    grad_proj = lax.dot_general(
        grad_output, up_stack, contract_last, preferred_element_type=jnp.float32
    )
    act_proj = lax.dot_general(
        hidden, down_stack, contract_last, preferred_element_type=jnp.float32
    )
    rank_part = jnp.concatenate([select_jobs(grad_proj), select_jobs(act_proj)], axis=1).astype(
        jnp.bfloat16
    )
    rank_sum = lax.psum(rank_part.astype(jnp.float32), "grp")
    chip_count = lax.axis_size("chip")
    row_of_chip = chip_count // group_count
    chip = lax.axis_index("chip")
    group = lax.axis_index("grp")
    core = lax.axis_index("core")
    lane = chip % row_of_chip
    arrived = []
    for step in range(group_count):
        piece = lax.dynamic_index_in_dim(quarter, (lane + step) % group_count, 0, keepdims=False)
        pairs = []
        for g in range(group_count):
            for c in range(chip_count):
                for k in range(2):
                    z = c % row_of_chip
                    dest_chip = g * row_of_chip + (z + step) % group_count
                    dest_group = c // row_of_chip
                    pairs.append(((g * chip_count + c) * 2 + k, (dest_group * chip_count + dest_chip) * 2 + k))
        arrived.append(lax.ppermute(piece, ("grp", "chip", "core"), pairs))
    arrived = jnp.stack(arrived)
    order = (lane - jnp.arange(group_count)) % group_count
    base_grad = jnp.take(arrived, order, axis=0).transpose(1, 0, 2).reshape(tok_rows, -1)
    grad_rank = rank_sum[:, :ranks].astype(jnp.bfloat16)
    act_rank = rank_sum[:, ranks:].astype(jnp.bfloat16)
    grad_spread = (
        (member[:, :, None] * lax.optimization_barrier(grad_rank).astype(jnp.float32)[:, None, :])
        .reshape(tok_rows, job_slots * ranks)
        .astype(jnp.bfloat16)
    )
    adapter_term = (
        jnp.dot(grad_spread, down_stack, preferred_element_type=jnp.float32) * ADAPTER_SCALE
    )
    grad_hidden = (base_grad.astype(jnp.float32) + adapter_term).astype(jnp.bfloat16)

    all_positions = lax.broadcasted_iota(jnp.int32, (shard_count, tok_rows, job_slots), 1)
    all_ends = jnp.cumsum(job_count, axis=1)
    all_starts = all_ends - job_count
    member_all = (
        (all_positions >= all_starts[:, None, :]) & (all_positions < all_ends[:, None, :])
    ).astype(jnp.float32)
    weight_all = jnp.sum(tenant_table * weights[None, None, :], axis=2)
    rank_rows = jnp.concatenate([grad_rank, act_rank], axis=1)
    rank_all = lax.all_to_all(
        jnp.broadcast_to(rank_rows[None], (shard_count,) + rank_rows.shape),
        SEQ,
        split_axis=0,
        concat_axis=0,
        tiled=True,
    ).astype(jnp.float32).reshape(shard_count, tok_rows, 1, 2 * ranks)
    tenant_map = (
        tenant_table.reshape(shard_count * job_slots, tenant_total).astype(jnp.bfloat16)
    )

    def adapter_grad(rank_rows, columns):
        spread = (member_all[:, :, :, None] * rank_rows).astype(jnp.bfloat16)
        per_job = jnp.einsum(
            "stjr,stc->sjrc", spread, columns, preferred_element_type=jnp.float32
        )
        per_job = (per_job * weight_all[:, :, None, None]).astype(jnp.bfloat16)
        slab = per_job.shape[-1]
        return lax.dot_general(
            tenant_map,
            per_job.reshape(shard_count * job_slots, ranks * slab),
            contract_rows,
            preferred_element_type=jnp.float32,
        ).reshape(tenant_total, ranks, slab)

    grad_adapter_down = adapter_grad(rank_all[..., :ranks], hidden_cols)
    grad_adapter_up = adapter_grad(rank_all[..., ranks:], output_cols)
    return (grad_hidden, grad_adapter_down, grad_adapter_up)


SEQ = ("chip", "core")


def solution(mesh):
    chips = mesh.devices.reshape(mesh.shape["grp"], mesh.shape["seq"] // 2, 2)
    mesh = jax.sharding.Mesh(chips, ("grp", "chip", "core"))
    placed = (
        P(SEQ, "grp"),
        P(SEQ, "grp"),
        P(SEQ, "grp"),
        P(None, None, ("grp", "chip", "core")),
        P(None, None, ("grp", "chip", "core")),
        P(),
        P(),
    )
    return jax.shard_map(
        shards,
        mesh=mesh,
        in_specs=placed,
        out_specs=(P(SEQ, "grp"), P(None, None, ("grp", "chip", "core")), P(None, None, ("grp", "chip", "core"))),
        check_vma=False,
    )
```

```python
import jax
import jax.numpy as jnp
from jax import lax
from jax.sharding import PartitionSpec as P

ADAPTER_SCALE = 2.0


def shards(grad_output, hidden, down_weight, adapter_down, adapter_up, job_tenant, job_count):
    shard_index = lax.axis_index(SEQ)
    shard_count = lax.axis_size(SEQ)
    group_count = lax.axis_size("grp")
    tok_rows = grad_output.shape[0]
    job_slots = job_tenant.shape[1]
    ranks = adapter_down.shape[1]
    down_slab = adapter_down.shape[2]
    up_slab = adapter_up.shape[2]
    tenant_total = adapter_down.shape[0]
    contract_last = (((1,), (1,)), ((), ()))
    contract_rows = (((0,), (0,)), ((), ()))
    tenant_table = (
        job_tenant[:, :, None] == lax.broadcasted_iota(jnp.int32, (1, 1, tenant_total), 2)
    ).astype(jnp.float32)
    totals = jnp.sum(job_count.astype(jnp.float32)[:, :, None] * tenant_table, axis=(0, 1))
    weights = ADAPTER_SCALE / totals
    table_here = lax.dynamic_index_in_dim(tenant_table, shard_index, 0, keepdims=False)
    job_weights = jnp.sum(table_here * weights[None, :], axis=1)
    counts_here = lax.dynamic_index_in_dim(job_count, shard_index, 0, keepdims=False)
    run_ends = jnp.cumsum(counts_here)
    run_starts = run_ends - counts_here
    positions = lax.broadcasted_iota(jnp.int32, (tok_rows, job_slots), 0)
    member = ((positions >= run_starts[None, :]) & (positions < run_ends[None, :])).astype(
        jnp.float32
    )
    hidden_cols = lax.all_to_all(
        hidden.reshape(tok_rows, shard_count, down_slab), SEQ, split_axis=1, concat_axis=0, tiled=True
    ).reshape(shard_count, tok_rows, down_slab)
    output_cols = lax.all_to_all(
        grad_output.reshape(tok_rows, shard_count, up_slab), SEQ, split_axis=1, concat_axis=0, tiled=True
    ).reshape(shard_count, tok_rows, up_slab)
    chosen = job_tenant.T
    fetched_down, fetched_up = (
        lax.all_to_all(adapter_down[chosen], SEQ, split_axis=1, concat_axis=3, tiled=True),
        lax.all_to_all(adapter_up[chosen], SEQ, split_axis=1, concat_axis=3, tiled=True),
    )
    down_stack = fetched_down.reshape(job_slots * ranks, shard_count * down_slab)
    up_stack = fetched_up.reshape(job_slots * ranks, shard_count * up_slab)

    def select_jobs(projected):
        return jnp.sum(projected.reshape(tok_rows, job_slots, ranks) * member[:, :, None], axis=1)

    grad_proj = lax.dot_general(
        grad_output, up_stack, contract_last, preferred_element_type=jnp.float32
    )
    act_proj = lax.dot_general(
        hidden, down_stack, contract_last, preferred_element_type=jnp.float32
    )
    rank_part = jnp.concatenate([select_jobs(grad_proj), select_jobs(act_proj)], axis=1).astype(
        jnp.bfloat16
    )
    partner_weight = lax.ppermute(down_weight, "core", [(0, 1), (1, 0)])
    on_first_core = lax.axis_index("core") == 0
    weight_pair = jnp.concatenate(
        [
            jnp.where(on_first_core, down_weight, partner_weight),
            jnp.where(on_first_core, partner_weight, down_weight),
        ],
        axis=0,
    )
    tokens_same_core = lax.all_gather(grad_output, "chip", axis=0, tiled=True)
    rank_sum = lax.psum(rank_part.astype(jnp.float32), "grp")
    tokens_same_core, weight_pair, rank_sum = lax.optimization_barrier(
        (tokens_same_core, weight_pair, rank_sum)
    )
    partial_value = lax.dot_general(
        tokens_same_core, weight_pair, contract_last, preferred_element_type=jnp.float32
    )
    quarter = lax.psum_scatter(
        partial_value.astype(jnp.bfloat16), "grp", scatter_dimension=0, tiled=True
    )
    quarter = quarter.reshape(group_count, tok_rows, quarter.shape[1])
    quarter, hidden_cols, output_cols = lax.optimization_barrier(
        (quarter, hidden_cols, output_cols)
    )
    chip_count = lax.axis_size("chip")
    row_of_chip = chip_count // group_count
    chip = lax.axis_index("chip")
    group = lax.axis_index("grp")
    core = lax.axis_index("core")
    lane = chip % row_of_chip
    arrived = []
    for step in range(group_count):
        piece = lax.dynamic_index_in_dim(quarter, (lane + step) % group_count, 0, keepdims=False)
        pairs = []
        for g in range(group_count):
            for c in range(chip_count):
                for k in range(2):
                    z = c % row_of_chip
                    dest_chip = g * row_of_chip + (z + step) % group_count
                    dest_group = c // row_of_chip
                    pairs.append(((g * chip_count + c) * 2 + k, (dest_group * chip_count + dest_chip) * 2 + k))
        arrived.append(lax.ppermute(piece, ("grp", "chip", "core"), pairs))
    arrived = jnp.stack(arrived)
    order = (lane - jnp.arange(group_count)) % group_count
    base_grad = jnp.take(arrived, order, axis=0).transpose(1, 0, 2).reshape(tok_rows, -1)
    grad_rank = rank_sum[:, :ranks].astype(jnp.bfloat16)
    act_rank = rank_sum[:, ranks:].astype(jnp.bfloat16)
    grad_spread = (
        (member[:, :, None] * lax.optimization_barrier(grad_rank).astype(jnp.float32)[:, None, :])
        .reshape(tok_rows, job_slots * ranks)
        .astype(jnp.bfloat16)
    )
    adapter_term = (
        jnp.dot(grad_spread, down_stack, preferred_element_type=jnp.float32) * ADAPTER_SCALE
    )
    grad_hidden = (base_grad.astype(jnp.float32) + adapter_term).astype(jnp.bfloat16)

    all_positions = lax.broadcasted_iota(jnp.int32, (shard_count, tok_rows, job_slots), 1)
    all_ends = jnp.cumsum(job_count, axis=1)
    all_starts = all_ends - job_count
    member_all = (
        (all_positions >= all_starts[:, None, :]) & (all_positions < all_ends[:, None, :])
    ).astype(jnp.float32)
    weight_all = jnp.sum(tenant_table * weights[None, None, :], axis=2)
    rank_rows = jnp.concatenate([grad_rank, act_rank], axis=1)
    rank_all = lax.all_to_all(
        jnp.broadcast_to(rank_rows[None], (shard_count,) + rank_rows.shape),
        SEQ,
        split_axis=0,
        concat_axis=0,
        tiled=True,
    ).astype(jnp.float32).reshape(shard_count, tok_rows, 1, 2 * ranks)
    tenant_map = (
        tenant_table.reshape(shard_count * job_slots, tenant_total).astype(jnp.bfloat16)
    )

    def adapter_grad(rank_rows, columns):
        spread = (member_all[:, :, :, None] * rank_rows).astype(jnp.bfloat16)
        per_job = jnp.einsum(
            "stjr,stc->sjrc", spread, columns, preferred_element_type=jnp.float32
        )
        per_job = (per_job * weight_all[:, :, None, None]).astype(jnp.bfloat16)
        slab = per_job.shape[-1]
        return lax.dot_general(
            tenant_map,
            per_job.reshape(shard_count * job_slots, ranks * slab),
            contract_rows,
            preferred_element_type=jnp.float32,
        ).reshape(tenant_total, ranks, slab)

    grad_adapter_down = adapter_grad(rank_all[..., :ranks], hidden_cols)
    grad_adapter_up = adapter_grad(rank_all[..., ranks:], output_cols)
    return (grad_hidden, grad_adapter_down, grad_adapter_up)


SEQ = ("chip", "core")


def solution(mesh):
    chips = mesh.devices.reshape(mesh.shape["grp"], mesh.shape["seq"] // 2, 2)
    mesh = jax.sharding.Mesh(chips, ("grp", "chip", "core"))
    placed = (
        P(SEQ, "grp"),
        P(SEQ, "grp"),
        P(SEQ, "grp"),
        P(None, None, ("grp", "chip", "core")),
        P(None, None, ("grp", "chip", "core")),
        P(),
        P(),
    )
    return jax.shard_map(
        shards,
        mesh=mesh,
        in_specs=placed,
        out_specs=(P(SEQ, "grp"), P(None, None, ("grp", "chip", "core")), P(None, None, ("grp", "chip", "core"))),
        check_vma=False,
    )
```

```python
import jax
import jax.numpy as jnp
from jax import lax
from jax.sharding import PartitionSpec as P

ADAPTER_SCALE = 2.0


def shards(grad_output, hidden, down_weight, adapter_down, adapter_up, job_tenant, job_count):
    shard_index = lax.axis_index(SEQ)
    shard_count = lax.axis_size(SEQ)
    group_count = lax.axis_size("grp")
    tok_rows = grad_output.shape[0]
    job_slots = job_tenant.shape[1]
    ranks = adapter_down.shape[1]
    down_slab = adapter_down.shape[2]
    up_slab = adapter_up.shape[2]
    tenant_total = adapter_down.shape[0]
    contract_last = (((1,), (1,)), ((), ()))
    contract_rows = (((0,), (0,)), ((), ()))
    tenant_table = (
        job_tenant[:, :, None] == lax.broadcasted_iota(jnp.int32, (1, 1, tenant_total), 2)
    ).astype(jnp.float32)
    totals = jnp.sum(job_count.astype(jnp.float32)[:, :, None] * tenant_table, axis=(0, 1))
    weights = ADAPTER_SCALE / totals
    table_here = lax.dynamic_index_in_dim(tenant_table, shard_index, 0, keepdims=False)
    job_weights = jnp.sum(table_here * weights[None, :], axis=1)
    counts_here = lax.dynamic_index_in_dim(job_count, shard_index, 0, keepdims=False)
    run_ends = jnp.cumsum(counts_here)
    run_starts = run_ends - counts_here
    positions = lax.broadcasted_iota(jnp.int32, (tok_rows, job_slots), 0)
    member = ((positions >= run_starts[None, :]) & (positions < run_ends[None, :])).astype(
        jnp.float32
    )
    hidden_cols = lax.all_to_all(
        hidden.reshape(tok_rows, shard_count, down_slab), SEQ, split_axis=1, concat_axis=0, tiled=True
    ).reshape(shard_count, tok_rows, down_slab)
    output_cols = lax.all_to_all(
        grad_output.reshape(tok_rows, shard_count, up_slab), SEQ, split_axis=1, concat_axis=0, tiled=True
    ).reshape(shard_count, tok_rows, up_slab)
    chosen = job_tenant.T
    fetched_down, fetched_up = (
        lax.all_to_all(adapter_down[chosen], SEQ, split_axis=1, concat_axis=3, tiled=True),
        lax.all_to_all(adapter_up[chosen], SEQ, split_axis=1, concat_axis=3, tiled=True),
    )
    down_stack = fetched_down.reshape(job_slots * ranks, shard_count * down_slab)
    up_stack = fetched_up.reshape(job_slots * ranks, shard_count * up_slab)

    def select_jobs(projected):
        return jnp.sum(projected.reshape(tok_rows, job_slots, ranks) * member[:, :, None], axis=1)

    grad_proj = lax.dot_general(
        grad_output, up_stack, contract_last, preferred_element_type=jnp.float32
    )
    act_proj = lax.dot_general(
        hidden, down_stack, contract_last, preferred_element_type=jnp.float32
    )
    rank_part = jnp.concatenate([select_jobs(grad_proj), select_jobs(act_proj)], axis=1).astype(
        jnp.bfloat16
    )
    weight_pair = lax.all_gather(down_weight, "core", axis=0, tiled=True)
    tokens_same_core = lax.all_gather(grad_output, "chip", axis=0, tiled=True)
    rank_sum = lax.psum(rank_part.astype(jnp.float32), "grp")
    tokens_same_core, weight_pair, rank_sum = lax.optimization_barrier(
        (tokens_same_core, weight_pair, rank_sum)
    )
    half_rows = weight_pair.shape[0] // 2
    halves = []
    for half in range(2):
        partial_value = lax.dot_general(
            tokens_same_core,
            weight_pair[half * half_rows:(half + 1) * half_rows],
            contract_last,
            preferred_element_type=jnp.float32,
        )
        halves.append(
            lax.psum_scatter(
                partial_value.astype(jnp.bfloat16), "grp", scatter_dimension=0, tiled=True
            )
        )
    quarter = jnp.concatenate(halves, axis=1)
    quarter = quarter.reshape(group_count, tok_rows, quarter.shape[1])
    quarter, hidden_cols, output_cols = lax.optimization_barrier(
        (quarter, hidden_cols, output_cols)
    )
    chip_count = lax.axis_size("chip")
    row_of_chip = chip_count // group_count
    chip = lax.axis_index("chip")
    group = lax.axis_index("grp")
    core = lax.axis_index("core")
    lane = chip % row_of_chip
    arrived = []
    for step in range(group_count):
        piece = lax.dynamic_index_in_dim(quarter, (lane + step) % group_count, 0, keepdims=False)
        pairs = []
        for g in range(group_count):
            for c in range(chip_count):
                for k in range(2):
                    z = c % row_of_chip
                    dest_chip = g * row_of_chip + (z + step) % group_count
                    dest_group = c // row_of_chip
                    pairs.append(((g * chip_count + c) * 2 + k, (dest_group * chip_count + dest_chip) * 2 + k))
        arrived.append(lax.ppermute(piece, ("grp", "chip", "core"), pairs))
    arrived = jnp.stack(arrived)
    order = (lane - jnp.arange(group_count)) % group_count
    base_grad = jnp.take(arrived, order, axis=0).transpose(1, 0, 2).reshape(tok_rows, -1)
    grad_rank = rank_sum[:, :ranks].astype(jnp.bfloat16)
    act_rank = rank_sum[:, ranks:].astype(jnp.bfloat16)
    grad_spread = (
        (member[:, :, None] * lax.optimization_barrier(grad_rank).astype(jnp.float32)[:, None, :])
        .reshape(tok_rows, job_slots * ranks)
        .astype(jnp.bfloat16)
    )
    adapter_term = (
        jnp.dot(grad_spread, down_stack, preferred_element_type=jnp.float32) * ADAPTER_SCALE
    )
    grad_hidden = (base_grad.astype(jnp.float32) + adapter_term).astype(jnp.bfloat16)

    all_positions = lax.broadcasted_iota(jnp.int32, (shard_count, tok_rows, job_slots), 1)
    all_ends = jnp.cumsum(job_count, axis=1)
    all_starts = all_ends - job_count
    member_all = (
        (all_positions >= all_starts[:, None, :]) & (all_positions < all_ends[:, None, :])
    ).astype(jnp.float32)
    weight_all = jnp.sum(tenant_table * weights[None, None, :], axis=2)
    rank_rows = jnp.concatenate([grad_rank, act_rank], axis=1)
    rank_all = lax.all_to_all(
        jnp.broadcast_to(rank_rows[None], (shard_count,) + rank_rows.shape),
        SEQ,
        split_axis=0,
        concat_axis=0,
        tiled=True,
    ).astype(jnp.float32).reshape(shard_count, tok_rows, 1, 2 * ranks)
    tenant_map = (
        tenant_table.reshape(shard_count * job_slots, tenant_total).astype(jnp.bfloat16)
    )

    def adapter_grad(rank_rows, columns):
        spread = (member_all[:, :, :, None] * rank_rows).astype(jnp.bfloat16)
        per_job = jnp.einsum(
            "stjr,stc->sjrc", spread, columns, preferred_element_type=jnp.float32
        )
        per_job = (per_job * weight_all[:, :, None, None]).astype(jnp.bfloat16)
        slab = per_job.shape[-1]
        return lax.dot_general(
            tenant_map,
            per_job.reshape(shard_count * job_slots, ranks * slab),
            contract_rows,
            preferred_element_type=jnp.float32,
        ).reshape(tenant_total, ranks, slab)

    grad_adapter_down = adapter_grad(rank_all[..., :ranks], hidden_cols)
    grad_adapter_up = adapter_grad(rank_all[..., ranks:], output_cols)
    return (grad_hidden, grad_adapter_down, grad_adapter_up)


SEQ = ("chip", "core")


def solution(mesh):
    chips = mesh.devices.reshape(mesh.shape["grp"], mesh.shape["seq"] // 2, 2)
    mesh = jax.sharding.Mesh(chips, ("grp", "chip", "core"))
    placed = (
        P(SEQ, "grp"),
        P(SEQ, "grp"),
        P(SEQ, "grp"),
        P(None, None, ("grp", "chip", "core")),
        P(None, None, ("grp", "chip", "core")),
        P(),
        P(),
    )
    return jax.shard_map(
        shards,
        mesh=mesh,
        in_specs=placed,
        out_specs=(P(SEQ, "grp"), P(None, None, ("grp", "chip", "core")), P(None, None, ("grp", "chip", "core"))),
        check_vma=False,
    )
```

```python
import jax
import jax.numpy as jnp
from jax import lax
from jax.sharding import PartitionSpec as P

ADAPTER_SCALE = 2.0


def shards(grad_output, hidden, down_weight, adapter_down, adapter_up, job_tenant, job_count):
    shard_index = lax.axis_index(SEQ)
    shard_count = lax.axis_size(SEQ)
    group_count = lax.axis_size("grp")
    tok_rows = grad_output.shape[0]
    job_slots = job_tenant.shape[1]
    ranks = adapter_down.shape[1]
    down_slab = adapter_down.shape[2]
    up_slab = adapter_up.shape[2]
    tenant_total = adapter_down.shape[0]
    contract_last = (((1,), (1,)), ((), ()))
    contract_rows = (((0,), (0,)), ((), ()))
    tenant_table = (
        job_tenant[:, :, None] == lax.broadcasted_iota(jnp.int32, (1, 1, tenant_total), 2)
    ).astype(jnp.float32)
    totals = jnp.sum(job_count.astype(jnp.float32)[:, :, None] * tenant_table, axis=(0, 1))
    weights = ADAPTER_SCALE / totals
    table_here = lax.dynamic_index_in_dim(tenant_table, shard_index, 0, keepdims=False)
    job_weights = jnp.sum(table_here * weights[None, :], axis=1)
    counts_here = lax.dynamic_index_in_dim(job_count, shard_index, 0, keepdims=False)
    run_ends = jnp.cumsum(counts_here)
    run_starts = run_ends - counts_here
    positions = lax.broadcasted_iota(jnp.int32, (tok_rows, job_slots), 0)
    member = ((positions >= run_starts[None, :]) & (positions < run_ends[None, :])).astype(
        jnp.float32
    )
    hidden_cols = lax.all_to_all(
        hidden.reshape(tok_rows, shard_count, down_slab), SEQ, split_axis=1, concat_axis=0, tiled=True
    ).reshape(shard_count, tok_rows, down_slab)
    output_cols = lax.all_to_all(
        grad_output.reshape(tok_rows, shard_count, up_slab), SEQ, split_axis=1, concat_axis=0, tiled=True
    ).reshape(shard_count, tok_rows, up_slab)
    chosen = job_tenant.T
    tokens_same_core = lax.all_gather(grad_output, "chip", axis=0, tiled=True)
    down_picked, tokens_same_core = lax.optimization_barrier((adapter_down[chosen], tokens_same_core))
    fetched_down, fetched_up = (
        lax.all_to_all(down_picked, SEQ, split_axis=1, concat_axis=3, tiled=True),
        lax.all_to_all(adapter_up[chosen], SEQ, split_axis=1, concat_axis=3, tiled=True),
    )
    down_stack = fetched_down.reshape(job_slots * ranks, shard_count * down_slab)
    up_stack = fetched_up.reshape(job_slots * ranks, shard_count * up_slab)

    def select_jobs(projected):
        return jnp.sum(projected.reshape(tok_rows, job_slots, ranks) * member[:, :, None], axis=1)

    grad_proj = lax.dot_general(
        grad_output, up_stack, contract_last, preferred_element_type=jnp.float32
    )
    act_proj = lax.dot_general(
        hidden, down_stack, contract_last, preferred_element_type=jnp.float32
    )
    rank_part = jnp.concatenate([select_jobs(grad_proj), select_jobs(act_proj)], axis=1).astype(
        jnp.bfloat16
    )
    weight_pair = lax.all_gather(down_weight, "core", axis=0, tiled=True)
    rank_sum = lax.psum(rank_part.astype(jnp.float32), "grp")
    partial_value = lax.dot_general(
        tokens_same_core, weight_pair, contract_last, preferred_element_type=jnp.float32
    )
    quarter = lax.psum_scatter(
        partial_value.astype(jnp.bfloat16), "grp", scatter_dimension=0, tiled=True
    )
    quarter = quarter.reshape(group_count, tok_rows, quarter.shape[1])
    quarter, hidden_cols, output_cols = lax.optimization_barrier(
        (quarter, hidden_cols, output_cols)
    )
    chip_count = lax.axis_size("chip")
    row_of_chip = chip_count // group_count
    chip = lax.axis_index("chip")
    group = lax.axis_index("grp")
    core = lax.axis_index("core")
    lane = chip % row_of_chip
    arrived = []
    for step in range(group_count):
        piece = lax.dynamic_index_in_dim(quarter, (lane + step) % group_count, 0, keepdims=False)
        pairs = []
        for g in range(group_count):
            for c in range(chip_count):
                for k in range(2):
                    z = c % row_of_chip
                    dest_chip = g * row_of_chip + (z + step) % group_count
                    dest_group = c // row_of_chip
                    pairs.append(((g * chip_count + c) * 2 + k, (dest_group * chip_count + dest_chip) * 2 + k))
        arrived.append(lax.ppermute(piece, ("grp", "chip", "core"), pairs))
    arrived = jnp.stack(arrived)
    order = (lane - jnp.arange(group_count)) % group_count
    base_grad = jnp.take(arrived, order, axis=0).transpose(1, 0, 2).reshape(tok_rows, -1)
    grad_rank = rank_sum[:, :ranks].astype(jnp.bfloat16)
    act_rank = rank_sum[:, ranks:].astype(jnp.bfloat16)
    grad_spread = (
        (member[:, :, None] * lax.optimization_barrier(grad_rank).astype(jnp.float32)[:, None, :])
        .reshape(tok_rows, job_slots * ranks)
        .astype(jnp.bfloat16)
    )
    adapter_term = (
        jnp.dot(grad_spread, down_stack, preferred_element_type=jnp.float32) * ADAPTER_SCALE
    )
    grad_hidden = (base_grad.astype(jnp.float32) + adapter_term).astype(jnp.bfloat16)

    all_positions = lax.broadcasted_iota(jnp.int32, (shard_count, tok_rows, job_slots), 1)
    all_ends = jnp.cumsum(job_count, axis=1)
    all_starts = all_ends - job_count
    member_all = (
        (all_positions >= all_starts[:, None, :]) & (all_positions < all_ends[:, None, :])
    ).astype(jnp.float32)
    weight_all = jnp.sum(tenant_table * weights[None, None, :], axis=2)
    rank_rows = jnp.concatenate([grad_rank, act_rank], axis=1)
    rank_all = lax.all_to_all(
        jnp.broadcast_to(rank_rows[None], (shard_count,) + rank_rows.shape),
        SEQ,
        split_axis=0,
        concat_axis=0,
        tiled=True,
    ).astype(jnp.float32).reshape(shard_count, tok_rows, 1, 2 * ranks)
    tenant_map = (
        tenant_table.reshape(shard_count * job_slots, tenant_total).astype(jnp.bfloat16)
    )

    def adapter_grad(rank_rows, columns):
        spread = (member_all[:, :, :, None] * rank_rows).astype(jnp.bfloat16)
        per_job = jnp.einsum(
            "stjr,stc->sjrc", spread, columns, preferred_element_type=jnp.float32
        )
        per_job = (per_job * weight_all[:, :, None, None]).astype(jnp.bfloat16)
        slab = per_job.shape[-1]
        return lax.dot_general(
            tenant_map,
            per_job.reshape(shard_count * job_slots, ranks * slab),
            contract_rows,
            preferred_element_type=jnp.float32,
        ).reshape(tenant_total, ranks, slab)

    grad_adapter_down = adapter_grad(rank_all[..., :ranks], hidden_cols)
    grad_adapter_up = adapter_grad(rank_all[..., ranks:], output_cols)
    return (grad_hidden, grad_adapter_down, grad_adapter_up)


SEQ = ("chip", "core")


def solution(mesh):
    chips = mesh.devices.reshape(mesh.shape["grp"], mesh.shape["seq"] // 2, 2)
    mesh = jax.sharding.Mesh(chips, ("grp", "chip", "core"))
    placed = (
        P(SEQ, "grp"),
        P(SEQ, "grp"),
        P(SEQ, "grp"),
        P(None, None, ("grp", "chip", "core")),
        P(None, None, ("grp", "chip", "core")),
        P(),
        P(),
    )
    return jax.shard_map(
        shards,
        mesh=mesh,
        in_specs=placed,
        out_specs=(P(SEQ, "grp"), P(None, None, ("grp", "chip", "core")), P(None, None, ("grp", "chip", "core"))),
        check_vma=False,
    )
```

```python
import jax
import jax.numpy as jnp
from jax import lax
from jax.sharding import PartitionSpec as P

ADAPTER_SCALE = 2.0


def shards(grad_output, hidden, down_weight, adapter_down, adapter_up, job_tenant, job_count):
    shard_index = lax.axis_index(SEQ)
    shard_count = lax.axis_size(SEQ)
    group_count = lax.axis_size("grp")
    tok_rows = grad_output.shape[0]
    job_slots = job_tenant.shape[1]
    ranks = adapter_down.shape[1]
    down_slab = adapter_down.shape[2]
    up_slab = adapter_up.shape[2]
    tenant_total = adapter_down.shape[0]
    contract_last = (((1,), (1,)), ((), ()))
    contract_rows = (((0,), (0,)), ((), ()))
    tenant_table = (
        job_tenant[:, :, None] == lax.broadcasted_iota(jnp.int32, (1, 1, tenant_total), 2)
    ).astype(jnp.float32)
    totals = jnp.sum(job_count.astype(jnp.float32)[:, :, None] * tenant_table, axis=(0, 1))
    weights = ADAPTER_SCALE / totals
    table_here = lax.dynamic_index_in_dim(tenant_table, shard_index, 0, keepdims=False)
    job_weights = jnp.sum(table_here * weights[None, :], axis=1)
    counts_here = lax.dynamic_index_in_dim(job_count, shard_index, 0, keepdims=False)
    run_ends = jnp.cumsum(counts_here)
    run_starts = run_ends - counts_here
    positions = lax.broadcasted_iota(jnp.int32, (tok_rows, job_slots), 0)
    member = ((positions >= run_starts[None, :]) & (positions < run_ends[None, :])).astype(
        jnp.float32
    )
    hidden_cols = lax.all_to_all(
        hidden.reshape(tok_rows, shard_count, down_slab), SEQ, split_axis=1, concat_axis=0, tiled=True
    ).reshape(shard_count, tok_rows, down_slab)
    output_cols = lax.all_to_all(
        grad_output.reshape(tok_rows, shard_count, up_slab), SEQ, split_axis=1, concat_axis=0, tiled=True
    ).reshape(shard_count, tok_rows, up_slab)
    chosen = job_tenant.T
    fetched_down, fetched_up = (
        lax.all_to_all(adapter_down[chosen], SEQ, split_axis=1, concat_axis=3, tiled=True),
        lax.all_to_all(adapter_up[chosen], SEQ, split_axis=1, concat_axis=3, tiled=True),
    )
    down_stack = fetched_down.reshape(job_slots * ranks, shard_count * down_slab)
    up_stack = fetched_up.reshape(job_slots * ranks, shard_count * up_slab)

    def select_jobs(projected):
        return jnp.sum(projected.reshape(tok_rows, job_slots, ranks) * member[:, :, None], axis=1)

    grad_proj = lax.dot_general(
        grad_output, up_stack, contract_last, preferred_element_type=jnp.float32
    )
    act_proj = lax.dot_general(
        hidden, down_stack, contract_last, preferred_element_type=jnp.float32
    )
    rank_part = jnp.concatenate([select_jobs(grad_proj), select_jobs(act_proj)], axis=1).astype(
        jnp.bfloat16
    )
    tokens_same_core = lax.all_gather(grad_output, "chip", axis=0, tiled=True)
    rank_sum = lax.psum(rank_part.astype(jnp.float32), "grp")
    tokens_same_core, rank_sum, weight_after = lax.optimization_barrier(
        (tokens_same_core, rank_sum, down_weight)
    )
    weight_pair = lax.all_gather(weight_after, "core", axis=0, tiled=True)
    own_core = lax.axis_index("core")
    weight_rows = down_weight.shape[0]
    partner_rows = lax.dynamic_slice_in_dim(weight_pair, (1 - own_core) * weight_rows, weight_rows, 0)
    partial_value = jnp.concatenate(
        [
            lax.dot_general(
                tokens_same_core, down_weight, contract_last, preferred_element_type=jnp.float32
            ),
            lax.dot_general(
                tokens_same_core, partner_rows, contract_last, preferred_element_type=jnp.float32
            ),
        ],
        axis=1,
    )
    quarter = lax.psum_scatter(
        partial_value.astype(jnp.bfloat16), "grp", scatter_dimension=0, tiled=True
    )
    quarter = quarter.reshape(group_count, tok_rows, quarter.shape[1])
    quarter, hidden_cols, output_cols = lax.optimization_barrier(
        (quarter, hidden_cols, output_cols)
    )
    chip_count = lax.axis_size("chip")
    row_of_chip = chip_count // group_count
    chip = lax.axis_index("chip")
    group = lax.axis_index("grp")
    core = lax.axis_index("core")
    lane = chip % row_of_chip
    arrived = []
    for step in range(group_count):
        piece = lax.dynamic_index_in_dim(quarter, (lane + step) % group_count, 0, keepdims=False)
        pairs = []
        for g in range(group_count):
            for c in range(chip_count):
                for k in range(2):
                    z = c % row_of_chip
                    dest_chip = g * row_of_chip + (z + step) % group_count
                    dest_group = c // row_of_chip
                    pairs.append(((g * chip_count + c) * 2 + k, (dest_group * chip_count + dest_chip) * 2 + k))
        arrived.append(lax.ppermute(piece, ("grp", "chip", "core"), pairs))
    arrived = jnp.stack(arrived)
    order = (lane - jnp.arange(group_count)) % group_count
    placed = jnp.take(arrived, order, axis=0).reshape(group_count, tok_rows, 2, weight_rows)
    placed = jnp.where(own_core == 0, placed, placed[:, :, ::-1, :])
    base_grad = placed.transpose(1, 0, 2, 3).reshape(tok_rows, -1)
    grad_rank = rank_sum[:, :ranks].astype(jnp.bfloat16)
    act_rank = rank_sum[:, ranks:].astype(jnp.bfloat16)
    grad_spread = (
        (member[:, :, None] * lax.optimization_barrier(grad_rank).astype(jnp.float32)[:, None, :])
        .reshape(tok_rows, job_slots * ranks)
        .astype(jnp.bfloat16)
    )
    adapter_term = (
        jnp.dot(grad_spread, down_stack, preferred_element_type=jnp.float32) * ADAPTER_SCALE
    )
    grad_hidden = (base_grad.astype(jnp.float32) + adapter_term).astype(jnp.bfloat16)

    all_positions = lax.broadcasted_iota(jnp.int32, (shard_count, tok_rows, job_slots), 1)
    all_ends = jnp.cumsum(job_count, axis=1)
    all_starts = all_ends - job_count
    member_all = (
        (all_positions >= all_starts[:, None, :]) & (all_positions < all_ends[:, None, :])
    ).astype(jnp.float32)
    weight_all = jnp.sum(tenant_table * weights[None, None, :], axis=2)
    rank_rows = jnp.concatenate([grad_rank, act_rank], axis=1)
    rank_all = lax.all_to_all(
        jnp.broadcast_to(rank_rows[None], (shard_count,) + rank_rows.shape),
        SEQ,
        split_axis=0,
        concat_axis=0,
        tiled=True,
    ).astype(jnp.float32).reshape(shard_count, tok_rows, 1, 2 * ranks)
    tenant_map = (
        tenant_table.reshape(shard_count * job_slots, tenant_total).astype(jnp.bfloat16)
    )

    def adapter_grad(rank_rows, columns):
        spread = (member_all[:, :, :, None] * rank_rows).astype(jnp.bfloat16)
        per_job = jnp.einsum(
            "stjr,stc->sjrc", spread, columns, preferred_element_type=jnp.float32
        )
        per_job = (per_job * weight_all[:, :, None, None]).astype(jnp.bfloat16)
        slab = per_job.shape[-1]
        return lax.dot_general(
            tenant_map,
            per_job.reshape(shard_count * job_slots, ranks * slab),
            contract_rows,
            preferred_element_type=jnp.float32,
        ).reshape(tenant_total, ranks, slab)

    grad_adapter_down = adapter_grad(rank_all[..., :ranks], hidden_cols)
    grad_adapter_up = adapter_grad(rank_all[..., ranks:], output_cols)
    return (grad_hidden, grad_adapter_down, grad_adapter_up)


SEQ = ("chip", "core")


def solution(mesh):
    chips = mesh.devices.reshape(mesh.shape["grp"], mesh.shape["seq"] // 2, 2)
    mesh = jax.sharding.Mesh(chips, ("grp", "chip", "core"))
    placed = (
        P(SEQ, "grp"),
        P(SEQ, "grp"),
        P(SEQ, "grp"),
        P(None, None, ("grp", "chip", "core")),
        P(None, None, ("grp", "chip", "core")),
        P(),
        P(),
    )
    return jax.shard_map(
        shards,
        mesh=mesh,
        in_specs=placed,
        out_specs=(P(SEQ, "grp"), P(None, None, ("grp", "chip", "core")), P(None, None, ("grp", "chip", "core"))),
        check_vma=False,
    )
```

```python
import jax
import jax.numpy as jnp
from jax import lax
from jax.sharding import PartitionSpec as P

ADAPTER_SCALE = 2.0


def shards(grad_output, hidden, down_weight, adapter_down, adapter_up, job_tenant, job_count):
    shard_index = lax.axis_index(SEQ)
    shard_count = lax.axis_size(SEQ)
    group_count = lax.axis_size("grp")
    tok_rows = grad_output.shape[0]
    job_slots = job_tenant.shape[1]
    ranks = adapter_down.shape[1]
    down_slab = adapter_down.shape[2]
    up_slab = adapter_up.shape[2]
    tenant_total = adapter_down.shape[0]
    contract_last = (((1,), (1,)), ((), ()))
    contract_rows = (((0,), (0,)), ((), ()))
    tenant_table = (
        job_tenant[:, :, None] == lax.broadcasted_iota(jnp.int32, (1, 1, tenant_total), 2)
    ).astype(jnp.float32)
    totals = jnp.sum(job_count.astype(jnp.float32)[:, :, None] * tenant_table, axis=(0, 1))
    weights = ADAPTER_SCALE / totals
    table_here = lax.dynamic_index_in_dim(tenant_table, shard_index, 0, keepdims=False)
    job_weights = jnp.sum(table_here * weights[None, :], axis=1)
    counts_here = lax.dynamic_index_in_dim(job_count, shard_index, 0, keepdims=False)
    run_ends = jnp.cumsum(counts_here)
    run_starts = run_ends - counts_here
    positions = lax.broadcasted_iota(jnp.int32, (tok_rows, job_slots), 0)
    member = ((positions >= run_starts[None, :]) & (positions < run_ends[None, :])).astype(
        jnp.float32
    )
    hidden_cols = lax.all_to_all(
        hidden.reshape(tok_rows, shard_count, down_slab), SEQ, split_axis=1, concat_axis=0, tiled=True
    ).reshape(shard_count, tok_rows, down_slab)
    output_cols = lax.all_to_all(
        grad_output.reshape(tok_rows, shard_count, up_slab), SEQ, split_axis=1, concat_axis=0, tiled=True
    ).reshape(shard_count, tok_rows, up_slab)
    chosen = job_tenant.T
    fetched_down, fetched_up = (
        lax.all_to_all(adapter_down[chosen], SEQ, split_axis=1, concat_axis=3, tiled=True),
        lax.all_to_all(adapter_up[chosen], SEQ, split_axis=1, concat_axis=3, tiled=True),
    )
    down_stack = fetched_down.reshape(job_slots * ranks, shard_count * down_slab)
    up_stack = fetched_up.reshape(job_slots * ranks, shard_count * up_slab)

    def select_jobs(projected):
        return jnp.sum(projected.reshape(tok_rows, job_slots, ranks) * member[:, :, None], axis=1)

    grad_proj = lax.dot_general(
        grad_output, up_stack, contract_last, preferred_element_type=jnp.float32
    )
    act_proj = lax.dot_general(
        hidden, down_stack, contract_last, preferred_element_type=jnp.float32
    )
    rank_part = jnp.concatenate([select_jobs(grad_proj), select_jobs(act_proj)], axis=1).astype(
        jnp.bfloat16
    )
    weight_pair = lax.all_gather(down_weight, "core", axis=0, tiled=True)
    tokens_same_core = lax.all_gather(grad_output, "chip", axis=0, tiled=True)
    rank_sum = lax.psum(rank_part.astype(jnp.float32), "grp")
    tokens_same_core, weight_pair, rank_sum = lax.optimization_barrier(
        (tokens_same_core, weight_pair, rank_sum)
    )
    partial_value = lax.dot_general(
        tokens_same_core, weight_pair, contract_last, preferred_element_type=jnp.float32
    )
    quarter = lax.psum_scatter(
        partial_value.astype(jnp.bfloat16), "grp", scatter_dimension=0, tiled=True
    )
    quarter = quarter.reshape(group_count, tok_rows, quarter.shape[1])
    quarter, hidden_cols, output_cols = lax.optimization_barrier(
        (quarter, hidden_cols, output_cols)
    )
    chip_count = lax.axis_size("chip")
    row_of_chip = chip_count // group_count
    chip = lax.axis_index("chip")
    group = lax.axis_index("grp")
    core = lax.axis_index("core")
    lane = chip % row_of_chip
    arrived = []
    for step in range(group_count):
        piece = lax.dynamic_index_in_dim(quarter, (lane + step) % group_count, 0, keepdims=False)
        pairs = []
        for g in range(group_count):
            for c in range(chip_count):
                for k in range(2):
                    z = c % row_of_chip
                    dest_chip = g * row_of_chip + (z + step) % group_count
                    dest_group = c // row_of_chip
                    pairs.append(((g * chip_count + c) * 2 + k, (dest_group * chip_count + dest_chip) * 2 + k))
        arrived.append(lax.ppermute(piece, ("grp", "chip", "core"), pairs))
    slots = []
    for z in range(group_count):
        source = (lane - z) % group_count
        piece = arrived[group_count - 1]
        for step in range(group_count - 2, -1, -1):
            piece = jnp.where(source == step, arrived[step], piece)
        slots.append(piece)
    base_grad = jnp.concatenate(slots, axis=1)
    grad_rank = rank_sum[:, :ranks].astype(jnp.bfloat16)
    act_rank = rank_sum[:, ranks:].astype(jnp.bfloat16)
    grad_spread = (
        (member[:, :, None] * lax.optimization_barrier(grad_rank).astype(jnp.float32)[:, None, :])
        .reshape(tok_rows, job_slots * ranks)
        .astype(jnp.bfloat16)
    )
    adapter_term = (
        jnp.dot(grad_spread, down_stack, preferred_element_type=jnp.float32) * ADAPTER_SCALE
    )
    grad_hidden = (base_grad.astype(jnp.float32) + adapter_term).astype(jnp.bfloat16)

    all_positions = lax.broadcasted_iota(jnp.int32, (shard_count, tok_rows, job_slots), 1)
    all_ends = jnp.cumsum(job_count, axis=1)
    all_starts = all_ends - job_count
    member_all = (
        (all_positions >= all_starts[:, None, :]) & (all_positions < all_ends[:, None, :])
    ).astype(jnp.float32)
    weight_all = jnp.sum(tenant_table * weights[None, None, :], axis=2)
    rank_rows = jnp.concatenate([grad_rank, act_rank], axis=1)
    rank_all = lax.all_to_all(
        jnp.broadcast_to(rank_rows[None], (shard_count,) + rank_rows.shape),
        SEQ,
        split_axis=0,
        concat_axis=0,
        tiled=True,
    ).astype(jnp.float32).reshape(shard_count, tok_rows, 1, 2 * ranks)
    tenant_map = (
        tenant_table.reshape(shard_count * job_slots, tenant_total).astype(jnp.bfloat16)
    )

    def adapter_grad(rank_rows, columns):
        spread = (member_all[:, :, :, None] * rank_rows).astype(jnp.bfloat16)
        per_job = jnp.einsum(
            "stjr,stc->sjrc", spread, columns, preferred_element_type=jnp.float32
        )
        per_job = (per_job * weight_all[:, :, None, None]).astype(jnp.bfloat16)
        slab = per_job.shape[-1]
        return lax.dot_general(
            tenant_map,
            per_job.reshape(shard_count * job_slots, ranks * slab),
            contract_rows,
            preferred_element_type=jnp.float32,
        ).reshape(tenant_total, ranks, slab)

    grad_adapter_down = adapter_grad(rank_all[..., :ranks], hidden_cols)
    grad_adapter_up = adapter_grad(rank_all[..., ranks:], output_cols)
    return (grad_hidden, grad_adapter_down, grad_adapter_up)


SEQ = ("chip", "core")


def solution(mesh):
    chips = mesh.devices.reshape(mesh.shape["grp"], mesh.shape["seq"] // 2, 2)
    mesh = jax.sharding.Mesh(chips, ("grp", "chip", "core"))
    placed = (
        P(SEQ, "grp"),
        P(SEQ, "grp"),
        P(SEQ, "grp"),
        P(None, None, ("grp", "chip", "core")),
        P(None, None, ("grp", "chip", "core")),
        P(),
        P(),
    )
    return jax.shard_map(
        shards,
        mesh=mesh,
        in_specs=placed,
        out_specs=(P(SEQ, "grp"), P(None, None, ("grp", "chip", "core")), P(None, None, ("grp", "chip", "core"))),
        check_vma=False,
    )
```

```python
import jax
import jax.numpy as jnp
from jax import lax
from jax.sharding import PartitionSpec as P

ADAPTER_SCALE = 2.0


def shards(grad_output, hidden, down_weight, adapter_down, adapter_up, job_tenant, job_count):
    shard_index = lax.axis_index(SEQ)
    shard_count = lax.axis_size(SEQ)
    group_count = lax.axis_size("grp")
    tok_rows = grad_output.shape[0]
    job_slots = job_tenant.shape[1]
    ranks = adapter_down.shape[1]
    down_slab = adapter_down.shape[2]
    up_slab = adapter_up.shape[2]
    tenant_total = adapter_down.shape[0]
    contract_last = (((1,), (1,)), ((), ()))
    contract_rows = (((0,), (0,)), ((), ()))
    tenant_table = (
        job_tenant[:, :, None] == lax.broadcasted_iota(jnp.int32, (1, 1, tenant_total), 2)
    ).astype(jnp.float32)
    totals = jnp.sum(job_count.astype(jnp.float32)[:, :, None] * tenant_table, axis=(0, 1))
    weights = ADAPTER_SCALE / totals
    table_here = lax.dynamic_index_in_dim(tenant_table, shard_index, 0, keepdims=False)
    job_weights = jnp.sum(table_here * weights[None, :], axis=1)
    counts_here = lax.dynamic_index_in_dim(job_count, shard_index, 0, keepdims=False)
    run_ends = jnp.cumsum(counts_here)
    run_starts = run_ends - counts_here
    positions = lax.broadcasted_iota(jnp.int32, (tok_rows, job_slots), 0)
    member = ((positions >= run_starts[None, :]) & (positions < run_ends[None, :])).astype(
        jnp.float32
    )
    hidden_cols = lax.all_to_all(
        hidden.reshape(tok_rows, shard_count, down_slab), SEQ, split_axis=1, concat_axis=0, tiled=True
    ).reshape(shard_count, tok_rows, down_slab)
    output_cols = lax.all_to_all(
        grad_output.reshape(tok_rows, shard_count, up_slab), SEQ, split_axis=1, concat_axis=0, tiled=True
    ).reshape(shard_count, tok_rows, up_slab)
    chosen = job_tenant.T
    fetched_down, fetched_up = (
        lax.all_to_all(adapter_down[chosen], SEQ, split_axis=1, concat_axis=3, tiled=True),
        lax.all_to_all(adapter_up[chosen], SEQ, split_axis=1, concat_axis=3, tiled=True),
    )
    down_stack = fetched_down.reshape(job_slots * ranks, shard_count * down_slab)
    up_stack = fetched_up.reshape(job_slots * ranks, shard_count * up_slab)

    def select_jobs(projected):
        return jnp.sum(projected.reshape(tok_rows, job_slots, ranks) * member[:, :, None], axis=1)

    grad_proj = lax.dot_general(
        grad_output, up_stack, contract_last, preferred_element_type=jnp.float32
    )
    act_proj = lax.dot_general(
        hidden, down_stack, contract_last, preferred_element_type=jnp.float32
    )
    rank_part = jnp.concatenate([select_jobs(grad_proj), select_jobs(act_proj)], axis=1).astype(
        jnp.bfloat16
    )
    weight_pair = lax.all_gather(down_weight, "core", axis=0, tiled=True)
    tokens_same_core = lax.all_gather(grad_output, "chip", axis=0, tiled=True)
    rank_sum = lax.psum(rank_part.astype(jnp.float32), "grp")
    tokens_same_core, weight_pair, rank_sum = lax.optimization_barrier(
        (tokens_same_core, weight_pair, rank_sum)
    )
    partial_value = lax.dot_general(
        tokens_same_core, weight_pair, contract_last, preferred_element_type=jnp.float32
    )
    quarter = lax.psum_scatter(
        partial_value.astype(jnp.bfloat16), "grp", scatter_dimension=0, tiled=True
    )
    quarter = quarter.reshape(group_count, tok_rows, quarter.shape[1])
    grad_rank = rank_sum[:, :ranks].astype(jnp.bfloat16)
    act_rank = rank_sum[:, ranks:].astype(jnp.bfloat16)
    all_positions = lax.broadcasted_iota(jnp.int32, (shard_count, tok_rows, job_slots), 1)
    all_ends = jnp.cumsum(job_count, axis=1)
    all_starts = all_ends - job_count
    member_all = (
        (all_positions >= all_starts[:, None, :]) & (all_positions < all_ends[:, None, :])
    ).astype(jnp.float32)
    weight_all = jnp.sum(tenant_table * weights[None, None, :], axis=2)
    rank_rows = jnp.concatenate([grad_rank, act_rank], axis=1)
    rank_all = lax.all_to_all(
        jnp.broadcast_to(rank_rows[None], (shard_count,) + rank_rows.shape),
        SEQ,
        split_axis=0,
        concat_axis=0,
        tiled=True,
    ).astype(jnp.float32).reshape(shard_count, tok_rows, 1, 2 * ranks)
    tenant_map = (
        tenant_table.reshape(shard_count * job_slots, tenant_total).astype(jnp.bfloat16)
    )

    def adapter_grad(rank_rows, columns):
        spread = (member_all[:, :, :, None] * rank_rows).astype(jnp.bfloat16)
        per_job = jnp.einsum(
            "stjr,stc->sjrc", spread, columns, preferred_element_type=jnp.float32
        )
        per_job = (per_job * weight_all[:, :, None, None]).astype(jnp.bfloat16)
        slab = per_job.shape[-1]
        return lax.dot_general(
            tenant_map,
            per_job.reshape(shard_count * job_slots, ranks * slab),
            contract_rows,
            preferred_element_type=jnp.float32,
        ).reshape(tenant_total, ranks, slab)

    grad_adapter_down = adapter_grad(rank_all[..., :ranks], hidden_cols)
    grad_adapter_up = adapter_grad(rank_all[..., ranks:], output_cols)
    grad_adapter_up, quarter = lax.optimization_barrier((grad_adapter_up, quarter))
    quarter, hidden_cols, output_cols = lax.optimization_barrier(
        (quarter, hidden_cols, output_cols)
    )
    chip_count = lax.axis_size("chip")
    row_of_chip = chip_count // group_count
    chip = lax.axis_index("chip")
    group = lax.axis_index("grp")
    core = lax.axis_index("core")
    lane = chip % row_of_chip
    arrived = []
    for step in range(group_count):
        piece = lax.dynamic_index_in_dim(quarter, (lane + step) % group_count, 0, keepdims=False)
        pairs = []
        for g in range(group_count):
            for c in range(chip_count):
                for k in range(2):
                    z = c % row_of_chip
                    dest_chip = g * row_of_chip + (z + step) % group_count
                    dest_group = c // row_of_chip
                    pairs.append(((g * chip_count + c) * 2 + k, (dest_group * chip_count + dest_chip) * 2 + k))
        arrived.append(lax.ppermute(piece, ("grp", "chip", "core"), pairs))
    slots = []
    for z in range(group_count):
        source = (lane - z) % group_count
        piece = arrived[group_count - 1]
        for step in range(group_count - 2, -1, -1):
            piece = jnp.where(source == step, arrived[step], piece)
        slots.append(piece)
    base_grad = jnp.concatenate(slots, axis=1)
    grad_spread = (
        (member[:, :, None] * lax.optimization_barrier(grad_rank).astype(jnp.float32)[:, None, :])
        .reshape(tok_rows, job_slots * ranks)
        .astype(jnp.bfloat16)
    )
    adapter_term = (
        jnp.dot(grad_spread, down_stack, preferred_element_type=jnp.float32) * ADAPTER_SCALE
    )
    grad_hidden = (base_grad.astype(jnp.float32) + adapter_term).astype(jnp.bfloat16)

    return (grad_hidden, grad_adapter_down, grad_adapter_up)


SEQ = ("chip", "core")


def solution(mesh):
    chips = mesh.devices.reshape(mesh.shape["grp"], mesh.shape["seq"] // 2, 2)
    mesh = jax.sharding.Mesh(chips, ("grp", "chip", "core"))
    placed = (
        P(SEQ, "grp"),
        P(SEQ, "grp"),
        P(SEQ, "grp"),
        P(None, None, ("grp", "chip", "core")),
        P(None, None, ("grp", "chip", "core")),
        P(),
        P(),
    )
    return jax.shard_map(
        shards,
        mesh=mesh,
        in_specs=placed,
        out_specs=(P(SEQ, "grp"), P(None, None, ("grp", "chip", "core")), P(None, None, ("grp", "chip", "core"))),
        check_vma=False,
    )
```

```python
import jax
import jax.numpy as jnp
from jax import lax
from jax.sharding import PartitionSpec as P

ADAPTER_SCALE = 2.0


def shards(grad_output, hidden, down_weight, adapter_down, adapter_up, job_tenant, job_count):
    shard_index = lax.axis_index(SEQ)
    shard_count = lax.axis_size(SEQ)
    group_count = lax.axis_size("grp")
    tok_rows = grad_output.shape[0]
    job_slots = job_tenant.shape[1]
    ranks = adapter_down.shape[1]
    down_slab = adapter_down.shape[2]
    up_slab = adapter_up.shape[2]
    tenant_total = adapter_down.shape[0]
    contract_last = (((1,), (1,)), ((), ()))
    contract_rows = (((0,), (0,)), ((), ()))
    tenant_table = (
        job_tenant[:, :, None] == lax.broadcasted_iota(jnp.int32, (1, 1, tenant_total), 2)
    ).astype(jnp.float32)
    totals = jnp.sum(job_count.astype(jnp.float32)[:, :, None] * tenant_table, axis=(0, 1))
    weights = ADAPTER_SCALE / totals
    table_here = lax.dynamic_index_in_dim(tenant_table, shard_index, 0, keepdims=False)
    job_weights = jnp.sum(table_here * weights[None, :], axis=1)
    counts_here = lax.dynamic_index_in_dim(job_count, shard_index, 0, keepdims=False)
    run_ends = jnp.cumsum(counts_here)
    run_starts = run_ends - counts_here
    positions = lax.broadcasted_iota(jnp.int32, (tok_rows, job_slots), 0)
    member = ((positions >= run_starts[None, :]) & (positions < run_ends[None, :])).astype(
        jnp.float32
    )
    hidden_cols = lax.all_to_all(
        hidden.reshape(tok_rows, shard_count, down_slab), SEQ, split_axis=1, concat_axis=0, tiled=True
    ).reshape(shard_count, tok_rows, down_slab)
    output_cols = lax.all_to_all(
        grad_output.reshape(tok_rows, shard_count, up_slab), SEQ, split_axis=1, concat_axis=0, tiled=True
    ).reshape(shard_count, tok_rows, up_slab)
    chosen = job_tenant.T
    tokens_same_core = lax.all_gather(grad_output, "chip", axis=0, tiled=True)
    down_picked, tokens_same_core = lax.optimization_barrier((adapter_down[chosen], tokens_same_core))
    fetched_down, fetched_up = (
        lax.all_to_all(down_picked, SEQ, split_axis=1, concat_axis=3, tiled=True),
        lax.all_to_all(adapter_up[chosen], SEQ, split_axis=1, concat_axis=3, tiled=True),
    )
    down_stack = fetched_down.reshape(job_slots * ranks, shard_count * down_slab)
    up_stack = fetched_up.reshape(job_slots * ranks, shard_count * up_slab)

    def select_jobs(projected):
        return jnp.sum(projected.reshape(tok_rows, job_slots, ranks) * member[:, :, None], axis=1)

    grad_proj = lax.dot_general(
        grad_output, up_stack, contract_last, preferred_element_type=jnp.float32
    )
    act_proj = lax.dot_general(
        hidden, down_stack, contract_last, preferred_element_type=jnp.float32
    )
    rank_part = jnp.concatenate([select_jobs(grad_proj), select_jobs(act_proj)], axis=1).astype(
        jnp.bfloat16
    )
    weight_pair = lax.all_gather(down_weight, "core", axis=0, tiled=True)
    rank_sum = lax.psum(rank_part.astype(jnp.float32), "grp")
    partial_value = lax.dot_general(
        tokens_same_core, weight_pair, contract_last, preferred_element_type=jnp.float32
    )
    quarter = lax.psum_scatter(
        partial_value.astype(jnp.bfloat16), "grp", scatter_dimension=0, tiled=True
    )
    quarter = quarter.reshape(group_count, tok_rows, quarter.shape[1])
    grad_rank = rank_sum[:, :ranks].astype(jnp.bfloat16)
    act_rank = rank_sum[:, ranks:].astype(jnp.bfloat16)
    all_positions = lax.broadcasted_iota(jnp.int32, (shard_count, tok_rows, job_slots), 1)
    all_ends = jnp.cumsum(job_count, axis=1)
    all_starts = all_ends - job_count
    member_all = (
        (all_positions >= all_starts[:, None, :]) & (all_positions < all_ends[:, None, :])
    ).astype(jnp.float32)
    weight_all = jnp.sum(tenant_table * weights[None, None, :], axis=2)
    rank_rows = jnp.concatenate([grad_rank, act_rank], axis=1)
    rank_all = lax.all_to_all(
        jnp.broadcast_to(rank_rows[None], (shard_count,) + rank_rows.shape),
        SEQ,
        split_axis=0,
        concat_axis=0,
        tiled=True,
    ).astype(jnp.float32).reshape(shard_count, tok_rows, 1, 2 * ranks)
    tenant_map = (
        tenant_table.reshape(shard_count * job_slots, tenant_total).astype(jnp.bfloat16)
    )

    def adapter_grad(rank_rows, columns):
        spread = (member_all[:, :, :, None] * rank_rows).astype(jnp.bfloat16)
        per_job = jnp.einsum(
            "stjr,stc->sjrc", spread, columns, preferred_element_type=jnp.float32
        )
        per_job = (per_job * weight_all[:, :, None, None]).astype(jnp.bfloat16)
        slab = per_job.shape[-1]
        return lax.dot_general(
            tenant_map,
            per_job.reshape(shard_count * job_slots, ranks * slab),
            contract_rows,
            preferred_element_type=jnp.float32,
        ).reshape(tenant_total, ranks, slab)

    grad_adapter_down = adapter_grad(rank_all[..., :ranks], hidden_cols)
    grad_adapter_up = adapter_grad(rank_all[..., ranks:], output_cols)
    grad_adapter_up, quarter = lax.optimization_barrier((grad_adapter_up, quarter))
    quarter, hidden_cols, output_cols = lax.optimization_barrier(
        (quarter, hidden_cols, output_cols)
    )
    chip_count = lax.axis_size("chip")
    row_of_chip = chip_count // group_count
    chip = lax.axis_index("chip")
    group = lax.axis_index("grp")
    core = lax.axis_index("core")
    lane = chip % row_of_chip
    arrived = []
    for step in range(group_count):
        piece = lax.dynamic_index_in_dim(quarter, (lane + step) % group_count, 0, keepdims=False)
        pairs = []
        for g in range(group_count):
            for c in range(chip_count):
                for k in range(2):
                    z = c % row_of_chip
                    dest_chip = g * row_of_chip + (z + step) % group_count
                    dest_group = c // row_of_chip
                    pairs.append(((g * chip_count + c) * 2 + k, (dest_group * chip_count + dest_chip) * 2 + k))
        arrived.append(lax.ppermute(piece, ("grp", "chip", "core"), pairs))
    slots = []
    for z in range(group_count):
        source = (lane - z) % group_count
        piece = arrived[group_count - 1]
        for step in range(group_count - 2, -1, -1):
            piece = jnp.where(source == step, arrived[step], piece)
        slots.append(piece)
    base_grad = jnp.concatenate(slots, axis=1)
    grad_spread = (
        (member[:, :, None] * lax.optimization_barrier(grad_rank).astype(jnp.float32)[:, None, :])
        .reshape(tok_rows, job_slots * ranks)
        .astype(jnp.bfloat16)
    )
    adapter_term = (
        jnp.dot(grad_spread, down_stack, preferred_element_type=jnp.float32) * ADAPTER_SCALE
    )
    grad_hidden = (base_grad.astype(jnp.float32) + adapter_term).astype(jnp.bfloat16)

    return (grad_hidden, grad_adapter_down, grad_adapter_up)


SEQ = ("chip", "core")


def solution(mesh):
    chips = mesh.devices.reshape(mesh.shape["grp"], mesh.shape["seq"] // 2, 2)
    mesh = jax.sharding.Mesh(chips, ("grp", "chip", "core"))
    placed = (
        P(SEQ, "grp"),
        P(SEQ, "grp"),
        P(SEQ, "grp"),
        P(None, None, ("grp", "chip", "core")),
        P(None, None, ("grp", "chip", "core")),
        P(),
        P(),
    )
    return jax.shard_map(
        shards,
        mesh=mesh,
        in_specs=placed,
        out_specs=(P(SEQ, "grp"), P(None, None, ("grp", "chip", "core")), P(None, None, ("grp", "chip", "core"))),
        check_vma=False,
    )
```
